128 devices in a mesh: seq: 16 (over z, y), head: 8 (over x, core).
Axes of the slice: x: 4, y: 4, z: 4, core: 2. Of those that a mesh axis runs over, the one named last changes fastest.
Arguments:
- hidden: bfloat16 [8192, 8192], P('seq'), may hold values from -6 to 6
- w_query: bfloat16 [8192, 4096], P('seq', 'head'), may hold values from -0.0625 to 0.0625
- w_key: bfloat16 [8192, 4096], P('seq', 'head'), may hold values from -0.0625 to 0.0625
- w_value: bfloat16 [8192, 4096], P('seq', 'head'), may hold values from -0.0625 to 0.0625
- cotangent: bfloat16 [8192, 4096], P('seq', 'head'), may hold values from -6 to 6
Outputs:
- step_direction: float32 [8192, 8192], P(('seq', 'head'))
The draws below stay inside these ranges and needn't reach their ends.
All inputs are finite; a program needn't handle non-finite values.
Results may differ from the reference program's by a relative error of at most 0.015.
Values may be sent and summed in bfloat16 or wider, within the bound.
No kernel may reach another device: no remote copies, remote signals or barrier semaphores. Data moves between devices by JAX's collectives and lax.ppermute only.
A program may use at most 192 MiB of HBM per device.

```python
import jax
import jax.numpy as jnp
from jax import lax

D = 8192
HEADS = 32
DH = 128
TOK_DEV = 512
TOKENS = 8192
N_HEAD = 8


def levels(key, extent, cuts, smallest, top_value):
    loudness = 1.0
    for dim, blocks in cuts:
        heights = jax.random.uniform(jax.random.fold_in(jax.random.fold_in(key, 6), dim), (blocks,), jnp.float32, smallest / len(cuts), top_value / len(cuts))
        loudness = loudness * jnp.repeat(jnp.exp(heights), extent[dim] // blocks).reshape((-1,) + (1,) * (len(extent) - 1 - dim))
    return loudness


def scatter_about(key, dims, spread, reach, split=(), dtype=jnp.bfloat16):
    drawn = spread * jax.random.normal(key, dims, jnp.float32)
    if split:
        drawn = drawn * levels(key, dims, split, -0.22, 0.18)
    return jnp.clip(drawn, -reach, reach).astype(dtype)


def setup_inputs(seed: int = 0) -> dict:
    keys = jax.random.split(jax.random.key(seed), 6)
    hidden = scatter_about(keys[0], (TOKENS, D), 1.0, 6.0, ((0, 16),))
    w_query = scatter_about(keys[1], (D, HEADS * DH), D ** -0.5, 0.0625, ((0, 16), (1, 8)))
    w_key = scatter_about(keys[2], (D, HEADS * DH), D ** -0.5, 0.0625, ((0, 16), (1, 8)))
    w_value = scatter_about(keys[3], (D, HEADS * DH), D ** -0.5, 0.0625, ((0, 16), (1, 8)))
    cotangent = scatter_about(keys[4], (TOKENS, HEADS * DH), 1.0, 6.0, ((0, 16), (1, 8)))
    return dict(hidden=hidden, w_query=w_query, w_key=w_key, w_value=w_value, cotangent=cotangent)


NORM_EPS = 1e-05
STEP_EPS = 1e-06

def silu_slope(preact):
    sigmoid = jax.nn.sigmoid(preact)
    return sigmoid * (1.0 + preact * (1.0 - sigmoid))

def reference(hidden, w_query, w_key, w_value, cotangent):
    col_total = w_query.shape[1]
    head_count = col_total // DH
    block_count = TOKENS // TOK_DEV
    pre_query = jnp.dot(hidden, w_query, preferred_element_type=jnp.float32)
    pre_key = jnp.dot(hidden, w_key, preferred_element_type=jnp.float32)
    pre_value = jnp.dot(hidden, w_value, preferred_element_type=jnp.float32)

    def blocked(matrix):
        return matrix.reshape(block_count, TOK_DEV, head_count, DH)
    query_rows = blocked(jax.nn.silu(pre_query).astype(jnp.bfloat16))
    key_rows = blocked(jax.nn.silu(pre_key).astype(jnp.bfloat16))
    value_rows = blocked(pre_value.astype(jnp.bfloat16))
    causal = (lax.broadcasted_iota(jnp.int32, (TOK_DEV, TOK_DEV), 0) >= lax.broadcasted_iota(jnp.int32, (TOK_DEV, TOK_DEV), 1))[None]

    def outer_sum(pair):
        return jnp.einsum('thi,thj->hij', pair[0].astype(jnp.float32), pair[1].astype(jnp.float32))
    own_states = lax.map(outer_sum, (key_rows, value_rows))
    zero_state = jnp.zeros_like(own_states[:1])
    before_all = jnp.concatenate([zero_state, jnp.cumsum(own_states, axis=0)[:-1]], axis=0)

    def block_scores(queries, keyed):
        scores = jnp.einsum('thd,shd->hts', queries.astype(jnp.float32), keyed.astype(jnp.float32))
        return jnp.where(causal, scores, 0.0).astype(jnp.bfloat16)

    def forward_block(parts):
        queries, keyed, valued, before = parts
        score_rows = block_scores(queries, keyed)
        inside = jnp.einsum('hts,shd->thd', score_rows.astype(jnp.float32), valued.astype(jnp.float32))
        carried = jnp.einsum('thi,hij->thj', queries.astype(jnp.float32), before, precision=lax.Precision.HIGHEST)
        return inside + carried
    attended = lax.map(forward_block, (query_rows, key_rows, value_rows, before_all))
    scale = lax.rsqrt(lax.optimization_barrier(jnp.mean(attended * attended, axis=-1, keepdims=True)) + NORM_EPS)
    normed = attended * scale
    upstream = blocked(cotangent.astype(jnp.float32))
    grad_att = (scale * (upstream - normed * lax.optimization_barrier(jnp.mean(upstream * normed, axis=-1, keepdims=True)))).astype(jnp.bfloat16)
    own_grads = lax.map(outer_sum, (query_rows, grad_att))
    inclusive = jnp.flip(jnp.cumsum(jnp.flip(own_grads, 0), axis=0), 0)
    after_all = jnp.concatenate([inclusive[1:], zero_state], axis=0)

    def backward_block(parts):
        queries, keyed, valued, grads, before, later_sum = parts
        score_rows = block_scores(queries, keyed).astype(jnp.float32)
        grad_scores = jnp.einsum('thd,shd->hts', grads.astype(jnp.float32), valued.astype(jnp.float32))
        grad_scores = jnp.where(causal, grad_scores, 0.0).astype(jnp.bfloat16).astype(jnp.float32)
        grad_query = jnp.einsum('hts,shd->thd', grad_scores, keyed.astype(jnp.float32)) + jnp.einsum('thj,hij->thi', grads.astype(jnp.float32), before, precision=lax.Precision.HIGHEST)
        grad_key = jnp.einsum('hts,thd->shd', grad_scores, queries.astype(jnp.float32)) + jnp.einsum('thj,hij->thi', valued.astype(jnp.float32), later_sum, precision=lax.Precision.HIGHEST)
        grad_value = jnp.einsum('hts,thd->shd', score_rows, grads.astype(jnp.float32)) + jnp.einsum('thi,hij->thj', keyed.astype(jnp.float32), later_sum, precision=lax.Precision.HIGHEST)
        return (grad_query, grad_key, grad_value)
    grad_query, grad_key, grad_value = lax.map(backward_block, (query_rows, key_rows, value_rows, grad_att, before_all, after_all))
    back_query = (grad_query.reshape(TOKENS, col_total) * silu_slope(pre_query)).astype(jnp.bfloat16)
    back_key = (grad_key.reshape(TOKENS, col_total) * silu_slope(pre_key)).astype(jnp.bfloat16)
    back_value = grad_value.reshape(TOKENS, col_total).astype(jnp.bfloat16)
    group_width = col_total // N_HEAD
    contract = (((1,), (1,)), ((), ()))
    input_grad = jnp.zeros((TOKENS, w_query.shape[0]), jnp.float32)
    for column_group in range(N_HEAD):
        columns = slice(column_group * group_width, (column_group + 1) * group_width)
        partial_value = lax.dot_general(back_query[:, columns], w_query[:, columns], contract, preferred_element_type=jnp.float32)
        partial_value = partial_value + lax.dot_general(back_key[:, columns], w_key[:, columns], contract, preferred_element_type=jnp.float32)
        partial_value = partial_value + lax.dot_general(back_value[:, columns], w_value[:, columns], contract, preferred_element_type=jnp.float32)
        rounded = lax.optimization_barrier(partial_value.astype(jnp.bfloat16))
        input_grad = input_grad + rounded.astype(jnp.float32)
    factor = lax.rsqrt(lax.optimization_barrier(jnp.mean(input_grad * input_grad, axis=-1, keepdims=True)) + STEP_EPS)
    return jnp.tanh(input_grad * factor)
```

```python
import jax
import jax.numpy as jnp
from jax import lax
from jax.experimental import pallas as pl
from jax.experimental.pallas import tpu as pltpu
from jax.sharding import Mesh
from jax.sharding import PartitionSpec as P

DH = 128
SEQ = ("z", "y")
HEAD = ("x", "c")
NORM_EPS = 1e-05
STEP_EPS = 1e-06
ORDERS = (
    (("z", 1), ("z", 3), ("y", 1), ("y", 3)),
    (("z", 3), ("z", 1), ("y", 3), ("y", 1)),
    (("y", 1), ("y", 3), ("z", 1), ("z", 3)),
    (("y", 3), ("y", 1), ("z", 3), ("z", 1)),
)
BF = jnp.bfloat16
F32 = jnp.float32


def swap(x, axis, offset):
    n = lax.axis_size(axis)
    return lax.ppermute(x, axis, [(i, i ^ offset) for i in range(n)])


def slot_offsets(order):
    slots = [(0, 0)]
    for axis, o in order:
        dz, dy = (o, 0) if axis == "z" else (0, o)
        slots = slots + [(z ^ dz, y ^ dy) for z, y in slots]
    return slots


def source_table():
    z, y = lax.axis_index("z"), lax.axis_index("y")
    rows = []
    for v, order in enumerate(ORDERS):
        rows.append(jnp.stack([((z ^ dz) * 4 + (y ^ dy)) * 4 + v for dz, dy in slot_offsets(order)]))
    return jnp.stack(rows).astype(jnp.int32)


def gather_quarter(rows, order):
    held = rows
    for axis, o in order[:-1]:
        held = jnp.concatenate([held, swap(held, axis, o)], axis=0)
    axis, o = order[-1]
    return held, swap(held, axis, o)


def gather_weight(block):
    quarter = block.shape[0] // 4
    return [gather_quarter(block[v * quarter : (v + 1) * quarter], order) for v, order in enumerate(ORDERS)]


def reorder_kernel(table, a, b, c, d, oa, ob, oc, od):
    oa[...] = a[...]
    ob[...] = b[...]
    oc[...] = c[...]
    od[...] = d[...]


def reorder_columns(hidden, table):
    rows, width = hidden.shape
    q = width // 64
    take = lambda v: pl.BlockSpec((rows, q), lambda k, t, v=v: (0, t[v, k]))
    give = pl.BlockSpec((rows, q), lambda k, t: (0, k))
    return pl.pallas_call(
        reorder_kernel,
        grid_spec=pltpu.PrefetchScalarGridSpec(
            num_scalar_prefetch=1, grid=(16,), in_specs=[take(v) for v in range(4)], out_specs=[give] * 4
        ),
        out_shape=[jax.ShapeDtypeStruct((rows, width // 4), hidden.dtype)] * 4,
        cost_estimate=pl.CostEstimate(flops=0, bytes_accessed=4 * rows * width, transcendentals=0),
        name="reorder_columns",
    )(table, hidden, hidden, hidden, hidden)


def finish_kernel(table, a, b, c, d, out):
    parts = (a, b, c, d)
    total = sum(jnp.sum(jnp.square(p[...].astype(F32)), axis=-1, keepdims=True) for p in parts)
    factor = lax.rsqrt(total / out.shape[1] + STEP_EPS)
    for v, p in enumerate(parts):
        for k in range(16):
            cols = pl.ds(pl.multiple_of(table[v, k] * 128, 128), 128)
            out[:, cols] = jnp.tanh(p[:, k * 128 : (k + 1) * 128].astype(F32) * factor)


def finish(parts, table):
    rows = parts[0].shape[0]
    width = 4 * parts[0].shape[1]
    return pl.pallas_call(
        finish_kernel,
        in_specs=[pl.BlockSpec(memory_space=pltpu.SMEM)] + [pl.BlockSpec(memory_space=pltpu.VMEM)] * 4,
        out_specs=pl.BlockSpec(memory_space=pltpu.VMEM),
        out_shape=jax.ShapeDtypeStruct((rows, width), F32),
        name="finish",
    )(table, *parts)


def states_over(own, reverse):
    total = own
    result = jnp.zeros_like(own)
    for axis in ("y", "z"):
        here = lax.axis_index(axis)
        sent = total.astype(BF)
        inside = jnp.zeros_like(own)
        for o in (1, 3, 2):
            other = swap(sent, axis, o).astype(F32)
            there = here ^ o
            inside = inside + jnp.where(there > here if reverse else there < here, other, 0.0)
            total = total + other
        result = result + inside
    return result


def silu_slope(preact):
    sigmoid = jax.nn.sigmoid(preact)
    return sigmoid * (1.0 + preact * (1.0 - sigmoid))


def row_order(first):
    second = 4 - first
    return [(ox, oc) for oc in (0, 1) for ox in (0, second, first, 2)]


def pick_rows(back, first):
    x, c = lax.axis_index("x"), lax.axis_index("c")
    groups = back.reshape(8, back.shape[0] // 8, back.shape[1])
    index = jnp.stack([(x ^ ox) * 2 + (c ^ oc) for ox, oc in row_order(first)])
    return jnp.concatenate([lax.dynamic_index_in_dim(groups, index[k], 0, False) for k in range(8)], axis=0)


def reduce_rows(mine, other, first):
    second = 4 - first
    got = swap(other, "c", 1)
    half = mine.shape[0] // 2
    send = (mine[half:] + got[half:].astype(F32)).astype(BF)
    got2 = swap(send, "x", first)
    keep = mine[:half] + got[:half].astype(F32) + got2.astype(F32)
    quarter = half // 2
    got3 = swap(keep[quarter:].astype(BF), "x", second)
    return keep[:quarter] + got3.astype(F32)


def on_device(hidden, w_query, w_key, w_value, cotangent):
    tok_rows = hidden.shape[0]
    col_width = w_query.shape[1]
    head_count = col_width // DH
    table = source_table()
    gathered_kv = gather_weight(jnp.concatenate([w_key, w_value], axis=1))
    gathered_q = gather_weight(w_query)
    hid = reorder_columns(hidden, table)

    def project(gathered):
        total = None
        for part in (0, 1):
            for v in range(4):
                w = gathered[v][part]
                depth = w.shape[0]
                term = jnp.dot(hid[v][:, part * depth : (part + 1) * depth], w, preferred_element_type=F32)
                total = term if total is None else total + term
        return total

    pre_kv = project(gathered_kv)
    pre_query = project(gathered_q)
    pre_key, pre_value = pre_kv[:, :col_width], pre_kv[:, col_width:]
    query_rows = jax.nn.silu(pre_query).astype(BF).reshape(tok_rows, head_count, DH)
    key_rows = jax.nn.silu(pre_key).astype(BF).reshape(tok_rows, head_count, DH)
    value_rows = pre_value.astype(BF).reshape(tok_rows, head_count, DH)
    causal = (
        lax.broadcasted_iota(jnp.int32, (tok_rows, tok_rows), 0)
        >= lax.broadcasted_iota(jnp.int32, (tok_rows, tok_rows), 1)
    )[None]
    own_state = jnp.einsum("thi,thj->hij", key_rows, value_rows, preferred_element_type=F32)
    before = states_over(own_state, False)
    scores = jnp.einsum("thd,shd->hts", query_rows, key_rows, preferred_element_type=F32)
    score_rows = jnp.where(causal, scores, 0.0).astype(BF)
    inside = jnp.einsum("hts,shd->thd", score_rows, value_rows, preferred_element_type=F32)
    carried = jnp.einsum("thi,hij->thj", query_rows.astype(F32), before)
    attended = inside + carried
    scale = lax.rsqrt(jnp.mean(attended * attended, axis=-1, keepdims=True) + NORM_EPS)
    normed = attended * scale
    upstream = cotangent.astype(F32).reshape(tok_rows, head_count, DH)
    grad_att = (
        scale * (upstream - normed * jnp.mean(upstream * normed, axis=-1, keepdims=True))
    ).astype(BF)
    own_grad = jnp.einsum("thi,thj->hij", query_rows, grad_att, preferred_element_type=F32)
    later_sum = states_over(own_grad, True)
    grad_scores = jnp.einsum("thd,shd->hts", grad_att, value_rows, preferred_element_type=F32)
    grad_scores = jnp.where(causal, grad_scores, 0.0).astype(BF)
    grad_query = jnp.einsum("hts,shd->thd", grad_scores, key_rows, preferred_element_type=F32) + jnp.einsum(
        "thj,hij->thi", grad_att.astype(F32), before
    )
    grad_key = jnp.einsum("hts,thd->shd", grad_scores, query_rows, preferred_element_type=F32) + jnp.einsum(
        "thj,hij->thi", value_rows.astype(F32), later_sum
    )
    grad_value = jnp.einsum("hts,thd->shd", score_rows, grad_att, preferred_element_type=F32) + jnp.einsum(
        "thi,hij->thj", key_rows.astype(F32), later_sum
    )
    back_query = (grad_query.reshape(tok_rows, col_width) * silu_slope(pre_query)).astype(BF)
    back_key = (grad_key.reshape(tok_rows, col_width) * silu_slope(pre_key)).astype(BF)
    back_value = grad_value.reshape(tok_rows, col_width).astype(BF)
    back = jnp.concatenate([back_key, back_value, back_query], axis=1)
    contract = (((1,), (1,)), ((), ()))
    parts = []
    ordered = {first: pick_rows(back, first) for first in (1, 3)}
    half = tok_rows // 2
    for v in range(4):
        first = 1 if v % 2 == 0 else 3
        rows = ordered[first]

        def push(r):
            cols = []
            for part in (0, 1):
                a = lax.dot_general(r[:, : 2 * col_width], gathered_kv[v][part], contract, preferred_element_type=F32)
                b = lax.dot_general(r[:, 2 * col_width :], gathered_q[v][part], contract, preferred_element_type=F32)
                cols.append(a + b)
            return jnp.concatenate(cols, axis=1)

        other = push(rows[half:]).astype(BF)
        mine = push(rows[:half])
        parts.append(reduce_rows(mine, other, first))
    return finish(parts, table)


def solution(mesh):
    finer = Mesh(mesh.devices.reshape(4, 4, 4, 2), ("z", "y", "x", "c"))
    in_specs = (P(SEQ, None), P(SEQ, HEAD), P(SEQ, HEAD), P(SEQ, HEAD), P(SEQ, HEAD))
    out_specs = P(SEQ + HEAD, None)
    return jax.shard_map(on_device, mesh=finer, in_specs=in_specs, out_specs=out_specs, check_vma=False)
```

```python
import functools

import jax
import jax.numpy as jnp
from jax import lax
from jax.experimental import pallas as pl
from jax.experimental.pallas import tpu as pltpu
from jax.sharding import Mesh
from jax.sharding import PartitionSpec as P

DH = 128
SEQ = ("z", "y")
HEAD = ("x", "c")
NORM_EPS = 1e-05
STEP_EPS = 1e-06
BF = jnp.bfloat16
F32 = jnp.float32
ORDERS = (
    ((("z", 1), ("z", 3), ("y", 1), ("y", 3)), (("z", 3), ("z", 1), ("y", 3), ("y", 1))),
    ((("y", 1), ("y", 3), ("z", 1), ("z", 3)), (("y", 3), ("y", 1), ("z", 3), ("z", 1))),
)
PLACES = (((0, 1, 2, 3, 4, 5, 6, 7), (0, 2, 1, 3, 4, 6, 5, 7)), ((0, 1, 2, 3, 4, 5, 6, 7), (4, 6, 5, 7, 0, 2, 1, 3)))
NT = (((1,), (1,)), ((), ()))
TN = (((0,), (0,)), ((), ()))


def swap(x, axis, offset):
    n = lax.axis_size(axis)
    return lax.ppermute(x, axis, [(i, i ^ offset) for i in range(n)])


def swap_links(x, half, step):
    pairs = []
    for z in range(4):
        for y in range(4):
            for c in range(2):
                axis, o = ORDERS[half][c][step]
                to_z, to_y = (z ^ o, y) if axis == "z" else (z, y ^ o)
                pairs.append(((z * 4 + y) * 2 + c, (to_z * 4 + to_y) * 2 + c))
    return lax.ppermute(x, ("z", "y", "c"), pairs)


def slot_offsets(order):
    slots = [(0, 0)]
    for axis, o in order:
        dz, dy = (o, 0) if axis == "z" else (0, o)
        slots = slots + [(z ^ dz, y ^ dy) for z, y in slots]
    return slots


def sources(half, core):
    z, y = lax.axis_index("z"), lax.axis_index("y")
    return jnp.stack([((z ^ dz) * 4 + (y ^ dy)) * 2 + half for dz, dy in slot_offsets(ORDERS[half][core])])


def own_sources():
    c = lax.axis_index("c")
    return jnp.stack([jnp.where(c == 0, sources(h, 0), sources(h, 1)) for h in (0, 1)]).astype(jnp.int32)


def after(x, *others):
    return lax.optimization_barrier((x, *others))[0]


def gather_phases(block):
    rows = block.shape[0] // 2
    held = [block[:rows], block[rows:]]
    for step in range(3):
        got = [swap_links(held[h], h, step) for h in (0, 1)]
        yield got
        held = [jnp.concatenate([held[h], got[h]], axis=0) for h in (0, 1)]
    got = [swap_links(held[h], h, 3) for h in (0, 1)]
    yield [(held[h], got[h]) for h in (0, 1)]


def reorder_kernel(table, a, b, oa, ob):
    oa[...] = a[...]
    ob[...] = b[...]


def reorder_columns(hidden, table):
    rows, width = hidden.shape
    q = width // 32
    take = lambda h: pl.BlockSpec((rows, q), lambda k, t, h=h: (0, t[h, k]))
    give = pl.BlockSpec((rows, q), lambda k, t: (0, k))
    return pl.pallas_call(
        reorder_kernel,
        grid_spec=pltpu.PrefetchScalarGridSpec(
            num_scalar_prefetch=1, grid=(16,), in_specs=[take(0), take(1)], out_specs=[give] * 2
        ),
        out_shape=[jax.ShapeDtypeStruct((rows, width // 2), hidden.dtype)] * 2,
        cost_estimate=pl.CostEstimate(flops=0, bytes_accessed=4 * rows * width, transcendentals=0),
        name="reorder_columns",
    )(table, hidden, hidden)


def finish_kernel(table, a, b, c, d, out):
    parts = (a, b, c, d)
    total = sum(jnp.sum(jnp.square(p[...].astype(F32)), axis=-1, keepdims=True) for p in parts)
    factor = lax.rsqrt(total / out.shape[1] + STEP_EPS)
    for v, p in enumerate(parts):
        for k in range(8):
            cols = pl.ds(pl.multiple_of(table[v * 8 + k] * 256, 256), 256)
            out[:, cols] = jnp.tanh(p[:, k * 256 : (k + 1) * 256].astype(F32) * factor)


def finish(parts, table):
    rows = parts[0].shape[0]
    width = 4 * parts[0].shape[1]
    return pl.pallas_call(
        finish_kernel,
        in_specs=[pl.BlockSpec(memory_space=pltpu.SMEM)] + [pl.BlockSpec(memory_space=pltpu.VMEM)] * 4,
        out_specs=pl.BlockSpec(memory_space=pltpu.VMEM),
        out_shape=jax.ShapeDtypeStruct((rows, width), F32),
        name="finish",
    )(table, *parts)


def states_over(own, reverse):
    total = own
    result = jnp.zeros_like(own)
    for axis in ("y", "z"):
        here = lax.axis_index(axis)
        sent = total.astype(BF)
        inside = jnp.zeros_like(own)
        for o in (1, 3, 2):
            other = swap(sent, axis, o).astype(F32)
            there = here ^ o
            inside = inside + jnp.where(there > here if reverse else there < here, other, 0.0)
            total = total + other
        result = result + inside
    return result


def sigmoid(a):
    return 1.0 / (1.0 + jnp.exp(-a))


def silu_slope(preact):
    gate = sigmoid(preact)
    return gate * (1.0 + preact * (1.0 - gate))


def dot(a, b, dims=(((1,), (0,)), ((), ()))):
    return lax.dot_general(a, b, dims, preferred_element_type=F32)


def attend_kernel(pre_q, pre_k, pre_v, before, cot, own_grad, back_q, grad_k, grad_v):
    pq = pre_q[...]
    pk = pre_k[...]
    q = (pq * sigmoid(pq)).astype(BF)
    k = (pk * sigmoid(pk)).astype(BF)
    v = pre_v[...].astype(BF)
    b = before[0].astype(BF)
    n = q.shape[0]
    causal = lax.broadcasted_iota(jnp.int32, (n, n), 0) >= lax.broadcasted_iota(jnp.int32, (n, n), 1)
    scores = jnp.where(causal, dot(q, k, NT), 0.0).astype(BF)
    attended = dot(scores, v) + dot(q, b)
    scale = lax.rsqrt(jnp.mean(attended * attended, axis=-1, keepdims=True) + NORM_EPS)
    normed = attended * scale
    up = cot[...].astype(F32)
    ga = (scale * (up - normed * jnp.mean(up * normed, axis=-1, keepdims=True))).astype(BF)
    own_grad[0] = dot(q, ga, TN)
    gs = jnp.where(causal, dot(ga, v, NT), 0.0).astype(BF)
    gq = dot(gs, k) + dot(ga, b, NT)
    back_q[...] = (gq * silu_slope(pq)).astype(BF)
    grad_k[...] = dot(gs, q, TN)
    grad_v[...] = dot(scores, ga, TN)


def attend(pre_query, pre_kv, before, cotangent):
    n, width = pre_query.shape
    heads = width // DH
    col = pl.BlockSpec((n, DH), lambda h: (0, h))
    col_v = pl.BlockSpec((n, DH), lambda h: (0, heads + h))
    state = pl.BlockSpec((1, DH, DH), lambda h: (h, 0, 0))
    return pl.pallas_call(
        attend_kernel,
        grid=(heads,),
        in_specs=[col, col, col_v, state, col],
        out_specs=[state, col, col, col],
        out_shape=[
            jax.ShapeDtypeStruct((heads, DH, DH), F32),
            jax.ShapeDtypeStruct((n, width), BF),
            jax.ShapeDtypeStruct((n, width), F32),
            jax.ShapeDtypeStruct((n, width), F32),
        ],
        name="attend",
    )(pre_query, pre_kv, pre_kv, before, cotangent)


def row_order(first):
    second = 4 - first
    return [(ox, oc) for oc in (1, 0) for ox in (0, second, first, 2)]


def collect_kernel(table, pre_kv, grad_k, grad_v, back_q, later, rows1, rows3, back):
    n, width = back_q.shape
    for h in range(width // DH):
        cols = slice(h * DH, (h + 1) * DH)
        vcols = slice(width + h * DH, width + (h + 1) * DH)
        pk = pre_kv[:, cols]
        k = (pk * sigmoid(pk)).astype(BF)
        v = pre_kv[:, vcols].astype(BF)
        a = later[h].astype(BF)
        back[:, cols] = ((grad_k[:, cols] + dot(v, a, NT)) * silu_slope(pk)).astype(BF)
        back[:, vcols] = (grad_v[:, cols] + dot(k, a)).astype(BF)
    back[:, 2 * width :] = back_q[...]
    g = n // 8
    for f, rows in enumerate((rows1, rows3)):
        for k in range(8):
            rows[k * g : (k + 1) * g, :] = back[pl.ds(pl.multiple_of(table[f * 8 + k] * g, g), g), :]


def collect(pre_kv, grad_k, grad_v, back_q, later):
    n, width = back_q.shape
    x, c = lax.axis_index("x"), lax.axis_index("c")
    table = jnp.stack([(x ^ ox) * 2 + (c ^ oc) for first in (1, 3) for ox, oc in row_order(first)]).astype(jnp.int32)
    return pl.pallas_call(
        collect_kernel,
        in_specs=[pl.BlockSpec(memory_space=pltpu.SMEM)] + [pl.BlockSpec(memory_space=pltpu.VMEM)] * 5,
        out_specs=[pl.BlockSpec(memory_space=pltpu.VMEM)] * 2,
        out_shape=[jax.ShapeDtypeStruct((n, 3 * width), BF)] * 2,
        scratch_shapes=[pltpu.VMEM((n, 3 * width), BF)],
        name="collect",
    )(table, pre_kv, grad_k, grad_v, back_q, later)


def push_kernel(places, rows, lo_kv, hi_kv, lo_q, hi_q, other, mine):
    i = pl.program_id(0)
    half = other.shape[0]
    wide = lo_kv.shape[1]

    def step(kv, q):
        r = dot(rows[:, :wide], kv[...], NT) + dot(rows[:, wide:], q[...], NT)
        for j in range(2):
            cols = pl.ds(pl.multiple_of(places[2 * i + j] * 256, 256), 256)
            other[:, cols] = r[:half, j * 256 : (j + 1) * 256].astype(other.dtype)
            mine[:, cols] = r[half:, j * 256 : (j + 1) * 256]

    @pl.when(i < 2)
    def _():
        step(lo_kv, lo_q)

    @pl.when(i >= 2)
    def _():
        step(hi_kv, hi_q)


def push(kind, rows, kv, q):
    n = rows.shape[0]
    places = jnp.where(lax.axis_index("c") == 0, jnp.array(PLACES[kind][0]), jnp.array(PLACES[kind][1])).astype(jnp.int32)
    lo_at, hi_at = (0, 2) if kind == 0 else (2, 0)
    lo = lambda a: pl.BlockSpec((512, a.shape[1]), lambda i, t: (lo_at + jnp.minimum(i, 1), 0))
    hi = lambda a: pl.BlockSpec((512, a.shape[1]), lambda i, t: (hi_at + jnp.maximum(i - 2, 0), 0))
    whole = lambda r, w: pl.BlockSpec((r, w), lambda i, t: (0, 0))
    return pl.pallas_call(
        push_kernel,
        grid_spec=pltpu.PrefetchScalarGridSpec(
            num_scalar_prefetch=1,
            grid=(4,),
            in_specs=[whole(*rows.shape), lo(kv[0]), hi(kv[1]), lo(q[0]), hi(q[1])],
            out_specs=[whole(n // 2, 2048), whole(n // 2, 2048)],
        ),
        out_shape=[jax.ShapeDtypeStruct((n // 2, 2048), BF), jax.ShapeDtypeStruct((n // 2, 2048), F32)],
        cost_estimate=pl.CostEstimate(flops=1000, bytes_accessed=1000, transcendentals=0),
        name="push",
    )(places, rows, kv[0], kv[1], q[0], q[1])


def on_device(hidden, w_query, w_key, w_value, cotangent):
    col_width = w_query.shape[1]
    heads = col_width // DH
    n = hidden.shape[0]
    hid = reorder_columns(hidden, own_sources())

    phases_kv = gather_phases(jnp.concatenate([w_key, w_value], axis=1))
    got = next(phases_kv)
    w_query = after(w_query, *got)
    phases_q = gather_phases(w_query)
    for step in range(1, 4):
        got_q = next(phases_q)
        got = next(phases_kv)
    kv = got
    q = next(phases_q)

    def project(gathered):
        total = None
        for part in (0, 1):
            for h in (0, 1):
                w = gathered[h][part]
                depth = w.shape[0]
                term = dot(hid[h][:, part * depth : (part + 1) * depth], w)
                total = term if total is None else total + term
        return total

    pre_kv = project(kv)
    pre_key, pre_value = pre_kv[:, :col_width], pre_kv[:, col_width:]
    key_rows = (pre_key * sigmoid(pre_key)).astype(BF).reshape(n, heads, DH)
    value_rows = pre_value.astype(BF).reshape(n, heads, DH)
    own_state = jnp.einsum("thi,thj->hij", key_rows, value_rows, preferred_element_type=F32)
    before = states_over(own_state, False)
    pre_query = project(q)
    own_grad, back_q, grad_k, grad_v = attend(pre_query, pre_kv, before, cotangent)
    later = states_over(own_grad, True)
    rows = collect(pre_kv, grad_k, grad_v, back_q, later)

    parts = []
    tables = []
    for h in (0, 1):
        for kind in (0, 1):
            first = (1, 3)[kind]
            second = 4 - first
            other, mine = push(kind, rows[kind], kv[h], q[h])
            got = swap(other, "c", 1)
            size = n // 8
            send = (mine[2 * size :] + got[2 * size :].astype(F32)).astype(BF)
            got2 = swap(send, "x", first)
            keep = mine[: 2 * size] + got[: 2 * size].astype(F32) + got2.astype(F32)
            got3 = swap(keep[size:].astype(BF), "x", second)
            parts.append(keep[:size] + got3.astype(F32))
            src = sources(h, 0)
            picks = (0, 1, 2, 3, 12, 13, 14, 15) if kind == 0 else (4, 5, 6, 7, 8, 9, 10, 11)
            tables.append(jnp.stack([src[p] for p in picks]))
    return finish(parts, jnp.concatenate(tables).astype(jnp.int32))


def solution(mesh):
    finer = Mesh(mesh.devices.reshape(4, 4, 4, 2), ("z", "y", "x", "c"))
    in_specs = (P(SEQ, None), P(SEQ, HEAD), P(SEQ, HEAD), P(SEQ, HEAD), P(SEQ, HEAD))
    out_specs = P(SEQ + HEAD, None)
    return jax.shard_map(on_device, mesh=finer, in_specs=in_specs, out_specs=out_specs, check_vma=False)
```

```python
import functools

import jax
import jax.numpy as jnp
from jax import lax
from jax.experimental import pallas as pl
from jax.experimental.pallas import tpu as pltpu
from jax.sharding import Mesh
from jax.sharding import PartitionSpec as P

DH = 128
SEQ = ("z", "y")
HEAD = ("x", "c")
NORM_EPS = 1e-05
STEP_EPS = 1e-06
BF = jnp.bfloat16
F32 = jnp.float32
ORDERS = (
    ((("z", 1), ("z", 3), ("y", 1), ("y", 3)), (("z", 3), ("z", 1), ("y", 3), ("y", 1))),
    ((("y", 1), ("y", 3), ("z", 1), ("z", 3)), (("y", 3), ("y", 1), ("z", 3), ("z", 1))),
)
NT = (((1,), (1,)), ((), ()))
TN = (((0,), (0,)), ((), ()))


def swap(x, axis, offset):
    n = lax.axis_size(axis)
    return lax.ppermute(x, axis, [(i, i ^ offset) for i in range(n)])


def swap_links(x, half, step):
    pairs = []
    for z in range(4):
        for y in range(4):
            for c in range(2):
                axis, o = ORDERS[half][c][step]
                to_z, to_y = (z ^ o, y) if axis == "z" else (z, y ^ o)
                pairs.append(((z * 4 + y) * 2 + c, (to_z * 4 + to_y) * 2 + c))
    return lax.ppermute(x, ("z", "y", "c"), pairs)


def slot_offsets(half, core):
    inner, outer = ORDERS[half][0][0][0], ORDERS[half][0][2][0]
    slots = []
    for group in (0, 1, 3, 2) if core == 0 else (0, 3, 1, 2):
        for o in (0, 1, 3, 2):
            offset = {inner: o, outer: group}
            slots.append((offset["z"], offset["y"]))
    return slots


def sources(half, core):
    z, y = lax.axis_index("z"), lax.axis_index("y")
    return jnp.stack([((z ^ dz) * 4 + (y ^ dy)) * 2 + half for dz, dy in slot_offsets(half, core)])


def own_sources():
    c = lax.axis_index("c")
    return jnp.stack([jnp.where(c == 0, sources(h, 0), sources(h, 1)) for h in (0, 1)]).astype(jnp.int32)


def after(x, *others):
    return lax.optimization_barrier((x, *others))[0]


def join(held, got, step):
    if step != 1:
        return jnp.concatenate([held, got], axis=0)
    n = 1
    first = lax.axis_index("c") == 0
    inner = [jnp.where(first, held[n:], got[:n]), jnp.where(first, got[:n], held[n:])]
    return jnp.concatenate([held[:n], *inner, got[n:]], axis=0)


def gather_two(block_a, block_b, ready):
    held_a, held_b = ([b[:1], b[1:]] for b in (block_a, block_b))
    got_a = [swap_links(held_a[h], h, 0) for h in (0, 1)]
    got_b = [swap_links(held_b[h], h, 0) for h in (0, 1)]
    for step in (0, 1, 2):
        wait = held_b if step < 2 else held_b + [*ready]
        held_a = [join(after(held_a[h], *wait), got_a[h], step) for h in (0, 1)]
        got_a = [swap_links(held_a[h], h, step + 1) for h in (0, 1)]
        held_b = [join(after(held_b[h], *held_a), got_b[h], step) for h in (0, 1)]
        got_b = [swap_links(held_b[h], h, step + 1) for h in (0, 1)]
    return (held_a, got_a), (held_b, got_b)


def reorder_kernel(table, a, b, oa, ob):
    oa[0] = a[...].T
    ob[0] = b[...].T


def reorder_columns(hidden, table):
    rows, width = hidden.shape
    q = width // 32
    take = lambda h: pl.BlockSpec((rows, q), lambda k, t, h=h: (0, t[h, k]))
    give = pl.BlockSpec((1, q, rows), lambda k, t: (k, 0, 0))
    return pl.pallas_call(
        reorder_kernel,
        grid_spec=pltpu.PrefetchScalarGridSpec(
            num_scalar_prefetch=1, grid=(16,), in_specs=[take(0), take(1)], out_specs=[give] * 2
        ),
        out_shape=[jax.ShapeDtypeStruct((16, q, rows), hidden.dtype)] * 2,
        cost_estimate=pl.CostEstimate(flops=0, bytes_accessed=4 * rows * width, transcendentals=0),
        name="reorder_columns",
    )(table, hidden, hidden)


def finish_kernel(table, a, b, c, d, out):
    parts = (a, b, c, d)
    total = sum(jnp.sum(jnp.square(p[...].astype(F32)), axis=-1, keepdims=True) for p in parts)
    factor = lax.rsqrt(total / out.shape[1] + STEP_EPS)
    for v, p in enumerate(parts):
        for k in range(8):
            cols = pl.ds(pl.multiple_of(table[v * 8 + k] * 256, 256), 256)
            out[:, cols] = jnp.tanh(p[:, k * 256 : (k + 1) * 256].astype(F32) * factor)


def finish(parts, table):
    rows = parts[0].shape[0]
    width = 4 * parts[0].shape[1]
    return pl.pallas_call(
        finish_kernel,
        in_specs=[pl.BlockSpec(memory_space=pltpu.SMEM)] + [pl.BlockSpec(memory_space=pltpu.VMEM)] * 4,
        out_specs=pl.BlockSpec(memory_space=pltpu.VMEM),
        out_shape=jax.ShapeDtypeStruct((rows, width), F32),
        name="finish",
    )(table, *parts)


def state_round(own, axis, reverse):
    here = lax.axis_index(axis)
    sent = own.astype(BF)
    inside = jnp.zeros_like(own)
    total = own
    for o in (1, 3, 2):
        other = swap(sent, axis, o).astype(F32)
        there = here ^ o
        inside = inside + jnp.where(there > here if reverse else there < here, other, 0.0)
        total = total + other
    return inside, total


def states_over(own, reverse):
    inner, total = state_round(own, "y", reverse)
    outer, _ = state_round(total, "z", reverse)
    return inner + outer


def sigmoid(a):
    return 1.0 / (1.0 + jnp.exp(-a))


def silu_slope(preact):
    gate = sigmoid(preact)
    return gate * (1.0 + preact * (1.0 - gate))


def dot(a, b, dims=(((1,), (0,)), ((), ()))):
    return lax.dot_general(a, b, dims, preferred_element_type=F32)


def causal_mask(n):
    return lax.broadcasted_iota(jnp.int32, (n, n), 0) <= lax.broadcasted_iota(jnp.int32, (n, n), 1)


def project_kernel(last, heads, *refs):
    first = 0 if last else 1
    start = refs[0] if last else None
    wa, wb, ha, hb, out = refs[1 - first : 6 - first]
    i = pl.program_id(0)

    def term(w, h):
        side = jnp.concatenate([w[k] for k in range(w.shape[0])], axis=1)
        return dot(side, h[...].reshape(-1, h.shape[2]))

    @pl.when(i == 0)
    def _():
        t = term(wa, ha)
        out[...] = start[...] + t if last else t

    @pl.when(i == 1)
    def _():
        out[...] += term(wa, ha)

    @pl.when(i >= 2)
    def _():
        out[...] += term(wb, hb)

    if heads:
        own = refs[-1]

        @pl.when(i == 3)
        def _():
            for h in range(heads):
                pk = out[h * DH : (h + 1) * DH, :]
                k = (pk * sigmoid(pk)).astype(BF)
                v = out[(heads + h) * DH : (heads + h + 1) * DH, :].astype(BF)
                own[h] = dot(k, v, NT)


def project(weights, hid, part, start, heads):
    cols, q = weights[0].shape[1:]
    n = hid[0].shape[2]
    last = start is not None
    lo = lambda i: jnp.minimum(i, 1)
    hi = lambda i: jnp.maximum(i - 2, 0)
    whole = pl.BlockSpec((cols, n), lambda i: (0, 0))
    in_specs = [
        pl.BlockSpec((4, cols, q), lambda i: (lo(i), 0, 0)),
        pl.BlockSpec((4, cols, q), lambda i: (hi(i), 0, 0)),
        pl.BlockSpec((4, q, n), lambda i: (2 * part + lo(i), 0, 0)),
        pl.BlockSpec((4, q, n), lambda i: (2 * part + hi(i), 0, 0)),
    ]
    out_specs = [whole]
    out_shape = [jax.ShapeDtypeStruct((cols, n), F32)]
    if heads:
        out_specs.append(pl.BlockSpec((heads, DH, DH), lambda i: (0, 0, 0)))
        out_shape.append(jax.ShapeDtypeStruct((heads, DH, DH), F32))
    got = pl.pallas_call(
        functools.partial(project_kernel, last, heads),
        grid=(4,),
        in_specs=([whole] if last else []) + in_specs,
        out_specs=out_specs,
        out_shape=out_shape,
        cost_estimate=pl.CostEstimate(flops=2 * 16 * cols * q * n, bytes_accessed=32 * (cols + n) * q, transcendentals=0),
        name="project",
    )(*([start] if last else []), *weights, *hid)
    return got if heads else got[0]


def attend_kernel(pre_q, pre_k, pre_v, before, cot, own_grad, grad_att, score):
    pq = pre_q[...]
    pk = pre_k[...]
    q = (pq * sigmoid(pq)).astype(BF)
    k = (pk * sigmoid(pk)).astype(BF)
    v = pre_v[...].astype(BF)
    b = before[0].astype(BF)
    scores = jnp.where(causal_mask(q.shape[1]), dot(k, q, TN), 0.0).astype(BF)
    score[0] = scores
    attended = dot(v, scores) + dot(b, q, TN)
    scale = lax.rsqrt(jnp.mean(attended * attended, axis=0, keepdims=True) + NORM_EPS)
    normed = attended * scale
    up = cot[...].T.astype(F32)
    ga = (scale * (up - normed * jnp.mean(up * normed, axis=0, keepdims=True))).astype(BF)
    grad_att[...] = ga
    own_grad[0] = dot(q, ga, NT)


def attend_back_kernel(pre_q, pre_k, pre_v, before, grad_att, score, back_q, grad_k, grad_v):
    pq = pre_q[...]
    pk = pre_k[...]
    q = (pq * sigmoid(pq)).astype(BF)
    k = (pk * sigmoid(pk)).astype(BF)
    v = pre_v[...].astype(BF)
    b = before[0].astype(BF)
    ga = grad_att[...]
    gs = jnp.where(causal_mask(q.shape[1]), dot(v, ga, TN), 0.0).astype(BF)
    gq = dot(k, gs) + dot(b, ga)
    back_q[...] = (gq * silu_slope(pq)).astype(BF)
    grad_k[...] = dot(q, gs, NT)
    grad_v[...] = dot(ga, score[0], NT)


def head_specs(n, heads):
    row = pl.BlockSpec((DH, n), lambda h: (h, 0))
    row_v = pl.BlockSpec((DH, n), lambda h: (heads + h, 0))
    state = pl.BlockSpec((1, DH, DH), lambda h: (h, 0, 0))
    square = pl.BlockSpec((1, n, n), lambda h: (h, 0, 0))
    return row, row_v, state, square


def attend(pre_query, pre_kv, before, cotangent):
    width, n = pre_query.shape
    heads = width // DH
    row, row_v, state, square = head_specs(n, heads)
    return pl.pallas_call(
        attend_kernel,
        grid=(heads,),
        in_specs=[row, row, row_v, state, pl.BlockSpec((n, DH), lambda h: (0, h))],
        out_specs=[state, row, square],
        out_shape=[
            jax.ShapeDtypeStruct((heads, DH, DH), F32),
            jax.ShapeDtypeStruct((width, n), BF),
            jax.ShapeDtypeStruct((heads, n, n), BF),
        ],
        name="attend",
    )(pre_query, pre_kv, pre_kv, before, cotangent)


def attend_back(pre_query, pre_kv, before, grad_att, score):
    width, n = pre_query.shape
    heads = width // DH
    row, row_v, state, square = head_specs(n, heads)
    return pl.pallas_call(
        attend_back_kernel,
        grid=(heads,),
        in_specs=[row, row, row_v, state, row, square],
        out_specs=[row, row, row],
        out_shape=[
            jax.ShapeDtypeStruct((width, n), BF),
            jax.ShapeDtypeStruct((width, n), F32),
            jax.ShapeDtypeStruct((width, n), F32),
        ],
        cost_estimate=pl.CostEstimate(flops=6 * heads * n * n * DH, bytes_accessed=16 * n * width, transcendentals=0),
        name="attend_back",
    )(pre_query, pre_kv, pre_kv, before, grad_att, score)


def row_order(first):
    second = 4 - first
    return [(ox, oc) for oc in (1, 0) for ox in (0, second, first, 2)]


def collect_kernel(table, pre_kv, grad_k, grad_v, back_q, later, rows1, rows3, back):
    width, n = back_q.shape
    for h in range(width // DH):
        cols = slice(h * DH, (h + 1) * DH)
        vcols = slice(width + h * DH, width + (h + 1) * DH)
        qcols = slice(2 * width + h * DH, 2 * width + (h + 1) * DH)
        pk = pre_kv[cols, :]
        k = (pk * sigmoid(pk)).astype(BF)
        v = pre_kv[vcols, :].astype(BF)
        a = later[h].astype(BF)
        back[:, cols] = ((grad_k[cols, :] + dot(a, v)) * silu_slope(pk)).astype(BF).T
        back[:, vcols] = (grad_v[cols, :] + dot(a, k, TN)).astype(BF).T
        back[:, qcols] = back_q[cols, :].T
    g = n // 8
    for f, rows in enumerate((rows1, rows3)):
        for k in range(8):
            rows[k * g : (k + 1) * g, :] = back[pl.ds(pl.multiple_of(table[f * 8 + k] * g, g), g), :]


def collect(pre_kv, grad_k, grad_v, back_q, later):
    width, n = back_q.shape
    x, c = lax.axis_index("x"), lax.axis_index("c")
    table = jnp.stack([(x ^ ox) * 2 + (c ^ oc) for first in (1, 3) for ox, oc in row_order(first)]).astype(jnp.int32)
    return pl.pallas_call(
        collect_kernel,
        in_specs=[pl.BlockSpec(memory_space=pltpu.SMEM)] + [pl.BlockSpec(memory_space=pltpu.VMEM)] * 5,
        out_specs=[pl.BlockSpec(memory_space=pltpu.VMEM)] * 2,
        out_shape=[jax.ShapeDtypeStruct((n, 3 * width), BF)] * 2,
        scratch_shapes=[pltpu.VMEM((n, 3 * width), BF)],
        name="collect",
    )(table, pre_kv, grad_k, grad_v, back_q, later)


def push_kernel(places, rows, kv_a, kv_b, q_a, q_b, other, mine):
    i = pl.program_id(0)
    half = other.shape[0]
    wide = kv_a.shape[1]
    cols = pl.ds(pl.multiple_of(places[i] * 1024, 1024), 1024)

    def step(kv, q):
        side = lambda w: jnp.concatenate([w[k] for k in range(4)], axis=1)
        kvs, qs = side(kv), side(q)
        r = dot(rows[:half, :wide], kvs) + dot(rows[:half, wide:], qs)
        other[:, cols] = r.astype(other.dtype)
        mine[:, cols] = dot(rows[half:, :wide], kvs) + dot(rows[half:, wide:], qs)

    @pl.when(i == 0)
    def _():
        step(kv_a, q_a)

    @pl.when(i == 1)
    def _():
        step(kv_b, q_b)


def push(kind, rows, kv, q):
    n = rows.shape[0]
    c = lax.axis_index("c")
    places = (jnp.stack([c, 1 - c]) if kind else jnp.array([0, 1])).astype(jnp.int32)
    lo, hi = ((0, 1), (1, 0))[kind]
    block = lambda a, at: pl.BlockSpec((4, *a.shape[1:]), lambda i, t, at=at: (at, 0, 0))
    whole = lambda r, w: pl.BlockSpec((r, w), lambda i, t: (0, 0))
    return pl.pallas_call(
        push_kernel,
        grid_spec=pltpu.PrefetchScalarGridSpec(
            num_scalar_prefetch=1,
            grid=(2,),
            in_specs=[whole(*rows.shape), block(kv[0], lo), block(kv[1], hi), block(q[0], lo), block(q[1], hi)],
            out_specs=[whole(n // 2, 2048), whole(n // 2, 2048)],
        ),
        out_shape=[jax.ShapeDtypeStruct((n // 2, 2048), BF), jax.ShapeDtypeStruct((n // 2, 2048), F32)],
        cost_estimate=pl.CostEstimate(flops=2 * n * 1536 * 2048, bytes_accessed=1536 * 4096, transcendentals=0),
        name="push",
    )(places, rows, kv[0], kv[1], q[0], q[1])


def transposed(w):
    return jnp.swapaxes(w.reshape(2, w.shape[0] // 2, w.shape[1]), 1, 2)


def on_device(hidden, w_query, w_key, w_value, cotangent):
    heads = w_query.shape[1] // DH
    n = hidden.shape[0]
    hid = reorder_columns(hidden, own_sources())
    w_kv = jnp.concatenate([transposed(w_key), transposed(w_value)], axis=1)
    (kv_lo, kv_hi), (q_lo, q_hi) = gather_two(w_kv, transposed(w_query), hid)
    kv = [(kv_lo[h], kv_hi[h]) for h in (0, 1)]
    q = [(q_lo[h], q_hi[h]) for h in (0, 1)]

    pre_kv = project(kv_lo, hid, 0, None, 0)
    pre_query = project(q_lo, hid, 0, None, 0)
    pre_kv, own_state = project(kv_hi, hid, 1, pre_kv, heads)
    inner, total = state_round(own_state, "y", False)
    outer, _ = state_round(total, "z", False)
    before = inner + outer
    pre_query = project(q_hi, [after(hid[0], total), hid[1]], 1, pre_query, 0)
    own_grad, grad_att, score = attend(pre_query, pre_kv, before, cotangent)
    back_q, grad_k, grad_v = attend_back(pre_query, pre_kv, before, grad_att, score)
    later = states_over(own_grad, True)
    rows = collect(pre_kv, grad_k, grad_v, back_q, later)

    parts = []
    tables = []
    started = []
    size = n // 8
    for h in (0, 1):
        for kind in (0, 1):
            first = (1, 3)[kind]
            second = 4 - first
            use = rows[kind]
            if len(started) >= 2:
                use = after(use, started[-2])
            other, mine = push(kind, use, kv[h], q[h])
            got = swap(other, "c", 1)
            send = (mine[2 * size :] + got[2 * size :].astype(F32)).astype(BF)
            started.append(send)
            got2 = swap(send, "x", first)
            keep = mine[: 2 * size] + got[: 2 * size].astype(F32) + got2.astype(F32)
            got3 = swap(keep[size:].astype(BF), "x", second)
            parts.append(keep[:size] + got3.astype(F32))
            src = sources(h, 0)
            picks = (0, 1, 2, 3, 12, 13, 14, 15) if kind == 0 else (4, 5, 6, 7, 8, 9, 10, 11)
            tables.append(jnp.stack([src[p] for p in picks]))
    return finish(parts, jnp.concatenate(tables).astype(jnp.int32))


def solution(mesh):
    finer = Mesh(mesh.devices.reshape(4, 4, 4, 2), ("z", "y", "x", "c"))
    in_specs = (P(SEQ, None), P(SEQ, HEAD), P(SEQ, HEAD), P(SEQ, HEAD), P(SEQ, HEAD))
    out_specs = P(SEQ + HEAD, None)
    return jax.shard_map(on_device, mesh=finer, in_specs=in_specs, out_specs=out_specs, check_vma=False)
```

```python
import functools

import jax
import jax.numpy as jnp
from jax import lax
from jax.experimental import pallas as pl
from jax.experimental.pallas import tpu as pltpu
from jax.sharding import Mesh
from jax.sharding import PartitionSpec as P

DH = 128
SEQ = ("z", "y")
HEAD = ("x", "c")
NORM_EPS = 1e-05
STEP_EPS = 1e-06
BF = jnp.bfloat16
F32 = jnp.float32
ORDERS = (
    ((("z", 1), ("z", 3), ("y", 1), ("y", 3)), (("z", 3), ("z", 1), ("y", 3), ("y", 1))),
    ((("y", 1), ("y", 3), ("z", 1), ("z", 3)), (("y", 3), ("y", 1), ("z", 3), ("z", 1))),
)
NT = (((1,), (1,)), ((), ()))
TN = (((0,), (0,)), ((), ()))


def swap(x, axis, offset):
    n = lax.axis_size(axis)
    return lax.ppermute(x, axis, [(i, i ^ offset) for i in range(n)])


def swap_links(x, half, step):
    pairs = []
    for z in range(4):
        for y in range(4):
            for c in range(2):
                axis, o = ORDERS[half][c][step]
                to_z, to_y = (z ^ o, y) if axis == "z" else (z, y ^ o)
                pairs.append(((z * 4 + y) * 2 + c, (to_z * 4 + to_y) * 2 + c))
    return lax.ppermute(x, ("z", "y", "c"), pairs)


def slot_offsets(half, core):
    inner, outer = ORDERS[half][0][0][0], ORDERS[half][0][2][0]
    slots = []
    for group in (0, 1, 3, 2) if core == 0 else (0, 3, 1, 2):
        for o in (0, 1, 3, 2):
            offset = {inner: o, outer: group}
            slots.append((offset["z"], offset["y"]))
    return slots


def sources(half, core):
    z, y = lax.axis_index("z"), lax.axis_index("y")
    return jnp.stack([((z ^ dz) * 4 + (y ^ dy)) * 2 + half for dz, dy in slot_offsets(half, core)])


def own_sources():
    c = lax.axis_index("c")
    return jnp.stack([jnp.where(c == 0, sources(h, 0), sources(h, 1)) for h in (0, 1)]).astype(jnp.int32)


def after(x, *others):
    return lax.optimization_barrier((x, *others))[0]


def join(held, got, step):
    if step != 1:
        return jnp.concatenate([held, got], axis=0)
    n = 1
    first = lax.axis_index("c") == 0
    inner = [jnp.where(first, held[n:], got[:n]), jnp.where(first, got[:n], held[n:])]
    return jnp.concatenate([held[:n], *inner, got[n:]], axis=0)


def gather_two(block_a, block_b, ready):
    held_a, held_b = ([b[:1], b[1:]] for b in (block_a, block_b))
    got_a = [swap_links(held_a[h], h, 0) for h in (0, 1)]
    got_b = [swap_links(held_b[h], h, 0) for h in (0, 1)]
    for step in (0, 1, 2):
        wait = held_b if step < 2 else held_b + [*ready]
        held_a = [join(after(held_a[h], *wait), got_a[h], step) for h in (0, 1)]
        got_a = [swap_links(held_a[h], h, step + 1) for h in (0, 1)]
        held_b = [join(after(held_b[h], *held_a), got_b[h], step) for h in (0, 1)]
        got_b = [swap_links(held_b[h], h, step + 1) for h in (0, 1)]
    return (held_a, got_a), (held_b, got_b)


def reorder_kernel(table, a, b, oa, ob):
    oa[0] = a[...].T
    ob[0] = b[...].T


def reorder_columns(hidden, table):
    rows, width = hidden.shape
    q = width // 32
    take = lambda h: pl.BlockSpec((rows, q), lambda k, t, h=h: (0, t[h, k]))
    give = pl.BlockSpec((1, q, rows), lambda k, t: (k, 0, 0))
    return pl.pallas_call(
        reorder_kernel,
        grid_spec=pltpu.PrefetchScalarGridSpec(
            num_scalar_prefetch=1, grid=(16,), in_specs=[take(0), take(1)], out_specs=[give] * 2
        ),
        out_shape=[jax.ShapeDtypeStruct((16, q, rows), hidden.dtype)] * 2,
        cost_estimate=pl.CostEstimate(flops=0, bytes_accessed=4 * rows * width, transcendentals=0),
        compiler_params=pltpu.CompilerParams(vmem_limit_bytes=8 << 20),
        name="reorder_columns",
    )(table, hidden, hidden)


def finish_kernel(table, a, b, c, d, out):
    parts = (a, b, c, d)
    total = sum(jnp.sum(jnp.square(p[...].astype(F32)), axis=-1, keepdims=True) for p in parts)
    factor = lax.rsqrt(total / out.shape[1] + STEP_EPS)
    for v, p in enumerate(parts):
        for k in range(8):
            cols = pl.ds(pl.multiple_of(table[v * 8 + k] * 256, 256), 256)
            out[:, cols] = jnp.tanh(p[:, k * 256 : (k + 1) * 256].astype(F32) * factor)


def finish(parts, table):
    rows = parts[0].shape[0]
    width = 4 * parts[0].shape[1]
    return pl.pallas_call(
        finish_kernel,
        in_specs=[pl.BlockSpec(memory_space=pltpu.SMEM)] + [pl.BlockSpec(memory_space=pltpu.VMEM)] * 4,
        out_specs=pl.BlockSpec(memory_space=pltpu.VMEM),
        out_shape=jax.ShapeDtypeStruct((rows, width), F32),
        compiler_params=pltpu.CompilerParams(vmem_limit_bytes=10 << 20),
        name="finish",
    )(table, *parts)


def state_round(own, axis, reverse):
    here = lax.axis_index(axis)
    sent = own.astype(BF)
    inside = jnp.zeros_like(own)
    total = own
    for o in (1, 3, 2):
        other = swap(sent, axis, o).astype(F32)
        there = here ^ o
        inside = inside + jnp.where(there > here if reverse else there < here, other, 0.0)
        total = total + other
    return inside, total


def states_over(own, reverse):
    inner, total = state_round(own, "y", reverse)
    outer, _ = state_round(total, "z", reverse)
    return inner + outer


def sigmoid(a):
    return 1.0 / (1.0 + jnp.exp(-a))


def silu_slope(preact):
    gate = sigmoid(preact)
    return gate * (1.0 + preact * (1.0 - gate))


def dot(a, b, dims=(((1,), (0,)), ((), ()))):
    return lax.dot_general(a, b, dims, preferred_element_type=F32)


def causal_mask(n):
    return lax.broadcasted_iota(jnp.int32, (n, n), 0) <= lax.broadcasted_iota(jnp.int32, (n, n), 1)


def side_by_side(w):
    return jnp.concatenate([w[k] for k in range(w.shape[0])], axis=1)


def project_kernel(part, last, heads, *refs):
    first = 1 if last else 0
    weights = refs[first : first + 2]
    hids = refs[first + 2 : first + 4]
    out = refs[first + 4]
    buf, sems = refs[-2:]
    copies = [
        pltpu.make_async_copy(weights[h].at[pl.ds(4 * g, 4)], buf.at[2 * h + g], sems.at[2 * h + g])
        for h in (0, 1)
        for g in (0, 1)
    ]
    copies[0].start()
    copies[1].start()
    for i in range(4):
        copies[i].wait()
        if i < 2:
            copies[i + 2].start()
        h = hids[i // 2]
        rows = h[8 * part + 4 * (i % 2) : 8 * part + 4 * (i % 2) + 4].reshape(-1, h.shape[2])
        t = dot(side_by_side(buf[i]), rows)
        if i:
            out[...] += t
        else:
            out[...] = refs[0][...] + t if last else t

    if heads:
        own = refs[first + 5]
        for h in range(heads):
            pk = out[h * DH : (h + 1) * DH, :]
            k = (pk * sigmoid(pk)).astype(BF)
            v = out[(heads + h) * DH : (heads + h + 1) * DH, :].astype(BF)
            own[h] = dot(k, v, NT)


def project(weights, hid, part, start, heads):
    cols, q = weights[0].shape[1:]
    n = hid[0].shape[2]
    last = start is not None
    vmem = pl.BlockSpec(memory_space=pltpu.VMEM)
    out_shape = [jax.ShapeDtypeStruct((cols, n), F32)]
    if heads:
        out_shape.append(jax.ShapeDtypeStruct((heads, DH, DH), F32))
    args = ([start] if last else []) + [*weights, *hid]
    got = pl.pallas_call(
        functools.partial(project_kernel, part, last, heads),
        in_specs=[vmem] * (1 if last else 0) + [pl.BlockSpec(memory_space=pl.ANY)] * 2 + [vmem] * 2,
        out_specs=[vmem] * len(out_shape),
        out_shape=out_shape,
        scratch_shapes=[pltpu.VMEM((4, 4, cols, q), BF), pltpu.SemaphoreType.DMA((4,))],
        cost_estimate=pl.CostEstimate(flops=2 * 16 * cols * q * n, bytes_accessed=32 * (cols + n) * q, transcendentals=0),
        compiler_params=pltpu.CompilerParams(vmem_limit_bytes=24 << 20),
        name="project",
    )(*args)
    return got if heads else got[0]


def attend_kernel(pre_q, pre_k, pre_v, before, cot, own_grad, grad_att, score):
    pq = pre_q[...]
    pk = pre_k[...]
    q = (pq * sigmoid(pq)).astype(BF)
    k = (pk * sigmoid(pk)).astype(BF)
    v = pre_v[...].astype(BF)
    b = before[0].astype(BF)
    scores = jnp.where(causal_mask(q.shape[1]), dot(k, q, TN), 0.0).astype(BF)
    score[0] = scores
    attended = dot(v, scores) + dot(b, q, TN)
    scale = lax.rsqrt(jnp.mean(attended * attended, axis=0, keepdims=True) + NORM_EPS)
    normed = attended * scale
    up = cot[...].T.astype(F32)
    ga = (scale * (up - normed * jnp.mean(up * normed, axis=0, keepdims=True))).astype(BF)
    grad_att[...] = ga
    own_grad[0] = dot(q, ga, NT)


def attend_back_kernel(pre_q, pre_k, pre_v, before, grad_att, score, back_q, grad_k, grad_v):
    pq = pre_q[...]
    pk = pre_k[...]
    q = (pq * sigmoid(pq)).astype(BF)
    k = (pk * sigmoid(pk)).astype(BF)
    v = pre_v[...].astype(BF)
    b = before[0].astype(BF)
    ga = grad_att[...]
    gs = jnp.where(causal_mask(q.shape[1]), dot(v, ga, TN), 0.0).astype(BF)
    gq = dot(k, gs) + dot(b, ga)
    back_q[...] = (gq * silu_slope(pq)).astype(BF)
    grad_k[...] = dot(q, gs, NT)
    grad_v[...] = dot(ga, score[0], NT)


def head_specs(n, heads):
    row = pl.BlockSpec((DH, n), lambda h: (h, 0))
    row_v = pl.BlockSpec((DH, n), lambda h: (heads + h, 0))
    state = pl.BlockSpec((1, DH, DH), lambda h: (h, 0, 0))
    square = pl.BlockSpec((1, n, n), lambda h: (h, 0, 0))
    return row, row_v, state, square


def attend(pre_query, pre_kv, before, cotangent):
    width, n = pre_query.shape
    heads = width // DH
    row, row_v, state, square = head_specs(n, heads)
    return pl.pallas_call(
        attend_kernel,
        grid=(heads,),
        in_specs=[row, row, row_v, state, pl.BlockSpec((n, DH), lambda h: (0, h))],
        out_specs=[state, row, square],
        out_shape=[
            jax.ShapeDtypeStruct((heads, DH, DH), F32),
            jax.ShapeDtypeStruct((width, n), BF),
            jax.ShapeDtypeStruct((heads, n, n), BF),
        ],
        compiler_params=pltpu.CompilerParams(vmem_limit_bytes=10 << 20),
        name="attend",
    )(pre_query, pre_kv, pre_kv, before, cotangent)


def attend_back(pre_query, pre_kv, before, grad_att, score):
    width, n = pre_query.shape
    heads = width // DH
    row, row_v, state, square = head_specs(n, heads)
    return pl.pallas_call(
        attend_back_kernel,
        grid=(heads,),
        in_specs=[row, row, row_v, state, row, square],
        out_specs=[row, row, row],
        out_shape=[
            jax.ShapeDtypeStruct((width, n), BF),
            jax.ShapeDtypeStruct((width, n), F32),
            jax.ShapeDtypeStruct((width, n), F32),
        ],
        cost_estimate=pl.CostEstimate(flops=6 * heads * n * n * DH, bytes_accessed=16 * n * width, transcendentals=0),
        compiler_params=pltpu.CompilerParams(vmem_limit_bytes=10 << 20),
        name="attend_back",
    )(pre_query, pre_kv, pre_kv, before, grad_att, score)


def row_order(first):
    second = 4 - first
    return [(ox, oc) for oc in (1, 0) for ox in (0, second, first, 2)]


def collect_kernel(table, pre_kv, grad_k, grad_v, back_q, later, rows1, rows3, back):
    width, n = back_q.shape
    for h in range(width // DH):
        cols = slice(h * DH, (h + 1) * DH)
        vcols = slice(width + h * DH, width + (h + 1) * DH)
        qcols = slice(2 * width + h * DH, 2 * width + (h + 1) * DH)
        pk = pre_kv[cols, :]
        k = (pk * sigmoid(pk)).astype(BF)
        v = pre_kv[vcols, :].astype(BF)
        a = later[h].astype(BF)
        back[:, cols] = ((grad_k[cols, :] + dot(a, v)) * silu_slope(pk)).astype(BF).T
        back[:, vcols] = (grad_v[cols, :] + dot(a, k, TN)).astype(BF).T
        back[:, qcols] = back_q[cols, :].T
    g = n // 8
    for f, rows in enumerate((rows1, rows3)):
        for k in range(8):
            rows[k * g : (k + 1) * g, :] = back[pl.ds(pl.multiple_of(table[f * 8 + k] * g, g), g), :]


def collect(pre_kv, grad_k, grad_v, back_q, later):
    width, n = back_q.shape
    x, c = lax.axis_index("x"), lax.axis_index("c")
    table = jnp.stack([(x ^ ox) * 2 + (c ^ oc) for first in (1, 3) for ox, oc in row_order(first)]).astype(jnp.int32)
    return pl.pallas_call(
        collect_kernel,
        in_specs=[pl.BlockSpec(memory_space=pltpu.SMEM)] + [pl.BlockSpec(memory_space=pltpu.VMEM)] * 5,
        out_specs=[pl.BlockSpec(memory_space=pltpu.VMEM)] * 2,
        out_shape=[jax.ShapeDtypeStruct((n, 3 * width), BF)] * 2,
        scratch_shapes=[pltpu.VMEM((n, 3 * width), BF)],
        compiler_params=pltpu.CompilerParams(vmem_limit_bytes=16 << 20),
        name="collect",
    )(table, pre_kv, grad_k, grad_v, back_q, later)


def push_kernel(groups, places, rows, kv_a, kv_b, q_a, q_b, other, mine, kv_buf, q_buf, sems):
    half = other.shape[0]
    wide = kv_a.shape[1]
    copies = []
    for i in range(4):
        kv, q = ((kv_a, q_a), (kv_b, q_b))[i // 2]
        at = pl.ds(groups[i // 2] + 2 * (i % 2), 2)
        copies.append(
            (
                pltpu.make_async_copy(kv.at[at], kv_buf.at[i], sems.at[i]),
                pltpu.make_async_copy(q.at[at], q_buf.at[i], sems.at[4 + i]),
            )
        )
    for i in (0, 1):
        for copy in copies[i]:
            copy.start()
    for i in range(4):
        for copy in copies[i]:
            copy.wait()
        if i < 2:
            for copy in copies[i + 2]:
                copy.start()
        cols = pl.ds(pl.multiple_of(places[i // 2] * 1024 + (i % 2) * 512, 512), 512)
        kvs, qs = side_by_side(kv_buf[i]), side_by_side(q_buf[i])
        other[:, cols] = (dot(rows[:half, :wide], kvs) + dot(rows[:half, wide:], qs)).astype(other.dtype)
        mine[:, cols] = dot(rows[half:, :wide], kvs) + dot(rows[half:, wide:], qs)


def push(kind, rows, kv, q):
    n = rows.shape[0]
    c = lax.axis_index("c")
    places = (jnp.stack([c, 1 - c]) if kind else jnp.array([0, 1])).astype(jnp.int32)
    vmem = pl.BlockSpec(memory_space=pltpu.VMEM)
    return pl.pallas_call(
        functools.partial(push_kernel, ((0, 4), (4, 0))[kind]),
        in_specs=[pl.BlockSpec(memory_space=pltpu.SMEM), vmem] + [pl.BlockSpec(memory_space=pl.ANY)] * 4,
        out_specs=[vmem] * 2,
        out_shape=[jax.ShapeDtypeStruct((n // 2, 2048), BF), jax.ShapeDtypeStruct((n // 2, 2048), F32)],
        scratch_shapes=[
            pltpu.VMEM((4, 2, *kv[0].shape[1:]), BF),
            pltpu.VMEM((4, 2, *q[0].shape[1:]), BF),
            pltpu.SemaphoreType.DMA((8,)),
        ],
        cost_estimate=pl.CostEstimate(flops=2 * n * 1536 * 2048, bytes_accessed=1536 * 4096, transcendentals=0),
        compiler_params=pltpu.CompilerParams(vmem_limit_bytes=24 << 20),
        name="push",
    )(places, rows, kv[0], kv[1], q[0], q[1])


def transposed(w):
    return jnp.swapaxes(w.reshape(2, w.shape[0] // 2, w.shape[1]), 1, 2)


def on_device(hidden, w_query, w_key, w_value, cotangent):
    heads = w_query.shape[1] // DH
    n = hidden.shape[0]
    hid = reorder_columns(hidden, own_sources())
    w_kv = jnp.concatenate([transposed(w_key), transposed(w_value)], axis=1)
    (kv_lo, kv_hi), (q_lo, q_hi) = gather_two(w_kv, transposed(w_query), hid)
    kv = [(kv_lo[h], kv_hi[h]) for h in (0, 1)]
    q = [(q_lo[h], q_hi[h]) for h in (0, 1)]

    pre_kv = project(kv_lo, hid, 0, None, 0)
    pre_query = project(q_lo, hid, 0, None, 0)
    pre_kv, own_state = project(kv_hi, hid, 1, pre_kv, heads)
    inner, total = state_round(own_state, "y", False)
    outer, _ = state_round(total, "z", False)
    before = inner + outer
    pre_query = project(q_hi, [after(hid[0], total), hid[1]], 1, pre_query, 0)
    own_grad, grad_att, score = attend(pre_query, pre_kv, before, cotangent)
    back_q, grad_k, grad_v = attend_back(pre_query, pre_kv, before, grad_att, score)
    later = states_over(own_grad, True)
    rows = collect(pre_kv, grad_k, grad_v, back_q, later)

    parts = []
    tables = []
    started = []
    size = n // 8
    for h in (0, 1):
        for kind in (0, 1):
            first = (1, 3)[kind]
            second = 4 - first
            use = rows[kind]
            if len(started) >= 2:
                use = after(use, started[-2])
            other, mine = push(kind, use, kv[h], q[h])
            got = swap(other, "c", 1)
            send = (mine[2 * size :] + got[2 * size :].astype(F32)).astype(BF)
            started.append(send)
            got2 = swap(send, "x", first)
            keep = mine[: 2 * size] + got[: 2 * size].astype(F32) + got2.astype(F32)
            got3 = swap(keep[size:].astype(BF), "x", second)
            parts.append(keep[:size] + got3.astype(F32))
            src = sources(h, 0)
            picks = (0, 1, 2, 3, 12, 13, 14, 15) if kind == 0 else (4, 5, 6, 7, 8, 9, 10, 11)
            tables.append(jnp.stack([src[p] for p in picks]))
    return finish(parts, jnp.concatenate(tables).astype(jnp.int32))


def solution(mesh):
    finer = Mesh(mesh.devices.reshape(4, 4, 4, 2), ("z", "y", "x", "c"))
    in_specs = (P(SEQ, None), P(SEQ, HEAD), P(SEQ, HEAD), P(SEQ, HEAD), P(SEQ, HEAD))
    out_specs = P(SEQ + HEAD, None)
    return jax.shard_map(on_device, mesh=finer, in_specs=in_specs, out_specs=out_specs, check_vma=False)
```

```python
import functools

import jax
import jax.numpy as jnp
from jax import lax
from jax.experimental import pallas as pl
from jax.experimental.pallas import tpu as pltpu
from jax.sharding import Mesh
from jax.sharding import PartitionSpec as P

DH = 128
SEQ = ("z", "y")
HEAD = ("x", "c")
NORM_EPS = 1e-05
STEP_EPS = 1e-06
BF = jnp.bfloat16
F32 = jnp.float32
ORDERS = (
    ((("z", 1), ("z", 3), ("y", 1), ("y", 3)), (("z", 3), ("z", 1), ("y", 3), ("y", 1))),
    ((("y", 1), ("y", 3), ("z", 1), ("z", 3)), (("y", 3), ("y", 1), ("z", 3), ("z", 1))),
)
PARTS = ((0, 8), (8, 12), (12, 16))
NT = (((1,), (1,)), ((), ()))
TN = (((0,), (0,)), ((), ()))


def swap(x, axis, offset):
    n = lax.axis_size(axis)
    return lax.ppermute(x, axis, [(i, i ^ offset) for i in range(n)])


def swap_links(x, half, step):
    pairs = []
    for z in range(4):
        for y in range(4):
            for c in range(2):
                axis, o = ORDERS[half][c][step]
                to_z, to_y = (z ^ o, y) if axis == "z" else (z, y ^ o)
                pairs.append(((z * 4 + y) * 2 + c, (to_z * 4 + to_y) * 2 + c))
    return lax.ppermute(x, ("z", "y", "c"), pairs)


def slot_offsets(half, core):
    inner, outer = ORDERS[half][0][0][0], ORDERS[half][0][2][0]
    slots = []
    for group in (0, 1, 3, 2) if core == 0 else (0, 3, 1, 2):
        for o in (0, 1, 3, 2):
            offset = {inner: o, outer: group}
            slots.append((offset["z"], offset["y"]))
    return slots


def sources(half, core):
    z, y = lax.axis_index("z"), lax.axis_index("y")
    return jnp.stack([((z ^ dz) * 4 + (y ^ dy)) * 2 + half for dz, dy in slot_offsets(half, core)])


def own_sources():
    c = lax.axis_index("c")
    return jnp.stack([jnp.where(c == 0, sources(h, 0), sources(h, 1)) for h in (0, 1)]).astype(jnp.int32)


def after(x, *others):
    return lax.optimization_barrier((x, *others))[0]


def join(held, got, step):
    if step != 1:
        return jnp.concatenate([held, got], axis=0)
    n = 1
    first = lax.axis_index("c") == 0
    inner = [jnp.where(first, held[n:], got[:n]), jnp.where(first, got[:n], held[n:])]
    return jnp.concatenate([held[:n], *inner, got[n:]], axis=0)


def gather(block, ready):
    held = [block[:1], block[1:]]
    for step in (0, 1):
        got = [swap_links(held[h], h, step) for h in (0, 1)]
        held = [join(held[h], got[h], step) for h in (0, 1)]
    near = [swap_links(held[h], h, 2) for h in (0, 1)]
    far = [swap_links(after(held[h], *ready), h, 3) for h in (0, 1)]
    wide = 2 * block.shape[1] // 3
    last_kv = [swap_links(near[h][:, :wide], h, 3) for h in (0, 1)]
    last_q = [swap_links(near[h][:, wide:], h, 3) for h in (0, 1)]
    return held, near, far, last_kv, last_q


def reorder_kernel(table, a, b, *outs):
    k = pl.program_id(0)
    for h, src in enumerate((a, b)):
        turned = src[...].T
        for p, (lo, hi) in enumerate(PARTS):

            @pl.when((k >= lo) & (k < hi))
            def _(out=outs[3 * h + p], turned=turned):
                out[0] = turned


def reorder_columns(hidden, table):
    rows, width = hidden.shape
    q = width // 32
    take = lambda h: pl.BlockSpec((rows, q), lambda k, t, h=h: (0, t[h, k]))
    give = [
        pl.BlockSpec((1, q, rows), lambda k, t, lo=lo, n=hi - lo: (jnp.clip(k - lo, 0, n - 1), 0, 0)) for lo, hi in PARTS
    ]
    return pl.pallas_call(
        reorder_kernel,
        grid_spec=pltpu.PrefetchScalarGridSpec(
            num_scalar_prefetch=1, grid=(16,), in_specs=[take(0), take(1)], out_specs=give * 2
        ),
        out_shape=[jax.ShapeDtypeStruct((hi - lo, q, rows), hidden.dtype) for lo, hi in PARTS] * 2,
        cost_estimate=pl.CostEstimate(flops=0, bytes_accessed=4 * rows * width, transcendentals=0),
        compiler_params=pltpu.CompilerParams(vmem_limit_bytes=2 << 20),
        name="reorder_columns",
    )(table, hidden, hidden)


def finish_kernel(table, a, b, c, d, out):
    parts = (a, b, c, d)
    total = sum(jnp.sum(jnp.square(p[...].astype(F32)), axis=-1, keepdims=True) for p in parts)
    factor = lax.rsqrt(total / out.shape[1] + STEP_EPS)
    for v, p in enumerate(parts):
        for k in range(8):
            cols = pl.ds(pl.multiple_of(table[v * 8 + k] * 256, 256), 256)
            out[:, cols] = jnp.tanh(p[:, k * 256 : (k + 1) * 256].astype(F32) * factor)


def finish(parts, table):
    rows = parts[0].shape[0]
    width = 4 * parts[0].shape[1]
    return pl.pallas_call(
        finish_kernel,
        in_specs=[pl.BlockSpec(memory_space=pltpu.SMEM)] + [pl.BlockSpec(memory_space=pltpu.VMEM)] * 4,
        out_specs=pl.BlockSpec(memory_space=pltpu.VMEM),
        out_shape=jax.ShapeDtypeStruct((rows, width), F32),
        compiler_params=pltpu.CompilerParams(vmem_limit_bytes=10 << 20),
        name="finish",
    )(table, *parts)


def state_round(own, axis, reverse):
    here = lax.axis_index(axis)
    sent = own.astype(BF)
    inside = jnp.zeros_like(own)
    total = own
    for o in (1, 3, 2):
        other = swap(sent, axis, o).astype(F32)
        there = here ^ o
        inside = inside + jnp.where(there > here if reverse else there < here, other, 0.0)
        total = total + other
    return inside, total


def sigmoid(a):
    return 1.0 / (1.0 + jnp.exp(-a))


def silu_slope(preact):
    gate = sigmoid(preact)
    return gate * (1.0 + preact * (1.0 - gate))


def dot(a, b, dims=(((1,), (0,)), ((), ()))):
    return lax.dot_general(a, b, dims, preferred_element_type=F32)


def causal_mask(n):
    return lax.broadcasted_iota(jnp.int32, (n, n), 0) <= lax.broadcasted_iota(jnp.int32, (n, n), 1)


def side_by_side(w):
    return jnp.concatenate([w[k] for k in range(w.shape[0])], axis=1)


def project_kernel(slots, starts, heads, *refs):
    count = len(slots)
    begins, refs = refs[:starts], refs[starts:]
    weights, hids, outs = refs[:count], refs[count : count + 2], refs[count + 2 : -3]
    buf, hid_buf, sems = refs[-3:]
    copies = []
    for i, (half, slot) in enumerate(slots):
        copies.append(pltpu.make_async_copy(weights[i], buf.at[i], sems.at[i]))
        copies.append(pltpu.make_async_copy(hids[half].at[pl.ds(slot, 4)], hid_buf.at[i], sems.at[count + i]))
    for copy in copies:
        copy.start()
    sums = outs[:-1] if heads else outs
    for i in range(count):
        copies[2 * i].wait()
        copies[2 * i + 1].wait()
        t = dot(side_by_side(buf[i]), hid_buf[i].reshape(-1, hid_buf.shape[3]))
        at = 0
        for j, out in enumerate(sums):
            part = t[at : at + out.shape[0]]
            at += out.shape[0]
            if i:
                out[...] += part
            else:
                out[...] = begins[j][...] + part if starts else part

    for h in range(heads):
        out = outs[0]
        pk = out[h * DH : (h + 1) * DH, :]
        k = (pk * sigmoid(pk)).astype(BF)
        v = out[(heads + h) * DH : (heads + h + 1) * DH, :].astype(BF)
        outs[-1][h] = dot(k, v, NT)


def project(limit, weights, slots, hid, widths, start=(), heads=0):
    cols, q = weights[0].shape[1:]
    n = hid[0].shape[2]
    vmem = pl.BlockSpec(memory_space=pltpu.VMEM)
    anywhere = pl.BlockSpec(memory_space=pltpu.HBM)
    out_shape = [jax.ShapeDtypeStruct((w, n), F32) for w in widths]
    if heads:
        out_shape.append(jax.ShapeDtypeStruct((heads, DH, DH), F32))
    count = len(slots)
    return pl.pallas_call(
        functools.partial(project_kernel, slots, len(start), heads),
        in_specs=[vmem] * len(start) + [anywhere] * (count + 2),
        out_specs=[vmem] * len(out_shape),
        out_shape=out_shape,
        scratch_shapes=[
            pltpu.VMEM((count, 4, cols, q), BF),
            pltpu.VMEM((count, 4, q, n), BF),
            pltpu.SemaphoreType.DMA((2 * count,)),
        ],
        cost_estimate=pl.CostEstimate(
            flops=8 * count * cols * q * n, bytes_accessed=8 * count * cols * q, transcendentals=0
        ),
        compiler_params=pltpu.CompilerParams(vmem_limit_bytes=limit << 20),
        name="project",
    )(*start, *weights, *hid)


def attend_kernel(pre_q, pre_k, pre_v, before, cot, own_grad, grad_att):
    pq = pre_q[...]
    pk = pre_k[...]
    q = (pq * sigmoid(pq)).astype(BF)
    k = (pk * sigmoid(pk)).astype(BF)
    v = pre_v[...].astype(BF)
    b = before[0].astype(BF)
    scores = jnp.where(causal_mask(q.shape[1]), dot(k, q, TN), 0.0).astype(BF)
    attended = dot(v, scores) + dot(b, q, TN)
    scale = lax.rsqrt(jnp.mean(attended * attended, axis=0, keepdims=True) + NORM_EPS)
    normed = attended * scale
    up = cot[...].T.astype(F32)
    ga = (scale * (up - normed * jnp.mean(up * normed, axis=0, keepdims=True))).astype(BF)
    grad_att[...] = ga
    own_grad[0] = dot(q, ga, NT)


def attend_back_kernel(pre_q, pre_k, pre_v, before, grad_att, back_q, grad_k, grad_v):
    pq = pre_q[...]
    pk = pre_k[...]
    q = (pq * sigmoid(pq)).astype(BF)
    k = (pk * sigmoid(pk)).astype(BF)
    v = pre_v[...].astype(BF)
    b = before[0].astype(BF)
    ga = grad_att[...]
    causal = causal_mask(q.shape[1])
    scores = jnp.where(causal, dot(k, q, TN), 0.0).astype(BF)
    gs = jnp.where(causal, dot(v, ga, TN), 0.0).astype(BF)
    gq = dot(k, gs) + dot(b, ga)
    back_q[...] = (gq * silu_slope(pq)).astype(BF)
    grad_k[...] = dot(q, gs, NT)
    grad_v[...] = dot(ga, scores, NT)


def head_specs(n, heads):
    row = pl.BlockSpec((DH, n), lambda h: (h, 0))
    row_v = pl.BlockSpec((DH, n), lambda h: (heads + h, 0))
    state = pl.BlockSpec((1, DH, DH), lambda h: (h, 0, 0))
    return row, row_v, state


def attend(pre_query, pre_kv, before, cotangent):
    width, n = pre_query.shape
    heads = width // DH
    row, row_v, state = head_specs(n, heads)
    return pl.pallas_call(
        attend_kernel,
        grid=(heads,),
        in_specs=[row, row, row_v, state, pl.BlockSpec((n, DH), lambda h: (0, h))],
        out_specs=[state, row],
        out_shape=[
            jax.ShapeDtypeStruct((heads, DH, DH), F32),
            jax.ShapeDtypeStruct((width, n), BF),
        ],
        compiler_params=pltpu.CompilerParams(vmem_limit_bytes=4 << 20),
        name="attend",
    )(pre_query, pre_kv, pre_kv, before, cotangent)


def attend_back(pre_query, pre_kv, before, grad_att):
    width, n = pre_query.shape
    heads = width // DH
    row, row_v, state = head_specs(n, heads)
    return pl.pallas_call(
        attend_back_kernel,
        grid=(heads,),
        in_specs=[row, row, row_v, state, row],
        out_specs=[row, row, row],
        out_shape=[
            jax.ShapeDtypeStruct((width, n), BF),
            jax.ShapeDtypeStruct((width, n), F32),
            jax.ShapeDtypeStruct((width, n), F32),
        ],
        cost_estimate=pl.CostEstimate(flops=6 * heads * n * n * DH, bytes_accessed=16 * n * width, transcendentals=0),
        compiler_params=pltpu.CompilerParams(vmem_limit_bytes=4 << 20),
        name="attend_back",
    )(pre_query, pre_kv, pre_kv, before, grad_att)


def row_order(first):
    second = 4 - first
    return [(ox, oc) for oc in (1, 0) for ox in (0, second, first, 2)]


def collect_kernel(table, pre_kv, grad_k, grad_v, back_q, later, rows1, rows3, back):
    width, n = back_q.shape
    for h in range(width // DH):
        cols = slice(h * DH, (h + 1) * DH)
        vcols = slice(width + h * DH, width + (h + 1) * DH)
        qcols = slice(2 * width + h * DH, 2 * width + (h + 1) * DH)
        pk = pre_kv[cols, :]
        k = (pk * sigmoid(pk)).astype(BF)
        v = pre_kv[vcols, :].astype(BF)
        a = later[h].astype(BF)
        back[:, cols] = ((grad_k[cols, :] + dot(a, v)) * silu_slope(pk)).astype(BF).T
        back[:, vcols] = (grad_v[cols, :] + dot(a, k, TN)).astype(BF).T
        back[:, qcols] = back_q[cols, :].T
    g = n // 8
    for f, rows in enumerate((rows1, rows3)):
        for k in range(8):
            rows[k * g : (k + 1) * g, :] = back[pl.ds(pl.multiple_of(table[f * 8 + k] * g, g), g), :]


def collect(pre_kv, grad_k, grad_v, back_q, later):
    width, n = back_q.shape
    x, c = lax.axis_index("x"), lax.axis_index("c")
    table = jnp.stack([(x ^ ox) * 2 + (c ^ oc) for first in (1, 3) for ox, oc in row_order(first)]).astype(jnp.int32)
    return pl.pallas_call(
        collect_kernel,
        in_specs=[pl.BlockSpec(memory_space=pltpu.SMEM)] + [pl.BlockSpec(memory_space=pltpu.VMEM)] * 5,
        out_specs=[pl.BlockSpec(memory_space=pltpu.VMEM)] * 2,
        out_shape=[jax.ShapeDtypeStruct((n, 3 * width), BF)] * 2,
        scratch_shapes=[pltpu.VMEM((n, 3 * width), BF)],
        compiler_params=pltpu.CompilerParams(vmem_limit_bytes=8 << 20),
        name="collect",
    )(table, pre_kv, grad_k, grad_v, back_q, later)


def push_kernel(kind, rows_in, *refs):
    count = 2 if kind else 3
    other, mine = refs[count : count + 2]
    rows = refs[count + 2]
    bufs = refs[count + 3 : 2 * count + 3]
    other_buf, mine_buf, sems, out_sems, rows_sem = refs[2 * count + 3 :]
    half = other.shape[0]
    c = lax.axis_index("c")
    places = (c, 1 - c) if kind else (0, 1)
    take_rows = pltpu.make_async_copy(rows_in, rows, rows_sem)
    take_rows.start()
    sides = [[(refs[0], bufs[0], 0)], [(refs[1], bufs[1], 0)]]
    if not kind:
        sides[1].append((refs[2], bufs[2], refs[1].shape[1]))
    copies = []
    for i in range(4):
        at = pl.ds(2 * (i % 2), 2)
        copies.append(
            [
                pltpu.make_async_copy(src.at[at], buf.at[at], sems.at[2 * i + j])
                for j, (src, buf, _) in enumerate(sides[i // 2])
            ]
        )
    for group in copies:
        for copy in group:
            copy.start()
    take_rows.wait()
    outs = []
    for i in range(4):
        for copy in copies[i]:
            copy.wait()
        total = None
        for _, buf, at in sides[i // 2]:
            side = jnp.concatenate([buf[2 * (i % 2)], buf[2 * (i % 2) + 1]], axis=1)
            term = dot(rows[:, at : at + side.shape[0]], side)
            total = term if total is None else total + term
        other_buf[i] = total[:half].astype(other.dtype)
        mine_buf[i] = total[half:].astype(mine.dtype)
        cols = pl.ds(pl.multiple_of(places[i // 2] * 1024 + (i % 2) * 512, 512), 512)
        for j, (buf, out) in enumerate(((other_buf, other), (mine_buf, mine))):
            outs.append(pltpu.make_async_copy(buf.at[i], out.at[:, cols], out_sems.at[2 * i + j]))
            outs[-1].start()
    for copy in outs:
        copy.wait()


def push(kind, rows, weights):
    n = rows.shape[0]
    hbm = pl.BlockSpec(memory_space=pltpu.HBM)
    return pl.pallas_call(
        functools.partial(push_kernel, kind),
        in_specs=[hbm] * (1 + len(weights)),
        out_specs=[hbm] * 2,
        out_shape=[jax.ShapeDtypeStruct((n // 2, 2048), BF)] * 2,
        scratch_shapes=[
            pltpu.VMEM(rows.shape, BF),
            *(pltpu.VMEM(w.shape, BF) for w in weights),
            pltpu.VMEM((4, n // 2, 512), BF),
            pltpu.VMEM((4, n // 2, 512), BF),
            pltpu.SemaphoreType.DMA((8,)),
            pltpu.SemaphoreType.DMA((8,)),
            pltpu.SemaphoreType.DMA,
        ],
        cost_estimate=pl.CostEstimate(flops=2 * n * 1536 * 2048, bytes_accessed=1536 * 4096, transcendentals=0),
        compiler_params=pltpu.CompilerParams(vmem_limit_bytes=54 << 20),
        name="push",
    )(rows, *weights)


def transposed(w):
    return jnp.swapaxes(w.reshape(2, w.shape[0] // 2, w.shape[1]), 1, 2)


def on_device(hidden, w_query, w_key, w_value, cotangent):
    heads = w_query.shape[1] // DH
    n = hidden.shape[0]
    hid = reorder_columns(hidden, own_sources())
    block = jnp.concatenate([transposed(w_key), transposed(w_value), transposed(w_query)], axis=1)
    held, near, far, last_kv, last_q = gather(block, hid)
    wide = 2 * heads * DH
    sums = project(20, [held[0], near[0], held[1], near[1]], ((0, 0), (0, 4), (1, 0), (1, 4)), hid[0::3], (wide, wide // 2))
    sums = project(14, far, ((0, 0), (1, 0)), hid[1::3], (wide, wide // 2), sums)
    pre_kv, own_state = project(44, last_kv, ((0, 0), (1, 0)), hid[2::3], (wide,), sums[:1], heads)
    inner, total = state_round(own_state, "y", False)
    outer, _ = state_round(total, "z", False)
    before = inner + outer
    pre_query = project(44, last_q, ((0, 0), (1, 0)), hid[2::3], (wide // 2,), sums[1:])[0]
    own_grad, grad_att = attend(pre_query, pre_kv, before, cotangent)
    back_q, grad_k, grad_v = attend_back(pre_query, pre_kv, before, grad_att)
    inner, total = state_round(own_grad, "y", True)
    outer, _ = state_round(after(total, back_q), "z", True)
    later = inner + outer
    rows = collect(pre_kv, grad_k, grad_v, back_q, later)

    size = n // 8
    tables = []
    started = []
    for h in (0, 1):
        for kind in (0, 1):
            use = rows[kind]
            if len(started) >= 2:
                use = after(use, started[-2][0])
            other, mine = push(kind, use, (near[h], far[h]) if kind else (held[h], last_kv[h], last_q[h]))
            got = swap(other, "c", 1)
            send = (mine[2 * size :].astype(F32) + got[2 * size :].astype(F32)).astype(BF)
            started.append((send, mine, got, swap(send, "x", (1, 3)[kind])))
            src = sources(h, 0)
            picks = (0, 1, 2, 3, 12, 13, 14, 15) if kind == 0 else (4, 5, 6, 7, 8, 9, 10, 11)
            tables.append(jnp.stack([src[p] for p in picks]))
    middle = []
    for i, (send, mine, got, got2) in enumerate(started):
        keep = mine[: 2 * size].astype(F32) + got[: 2 * size].astype(F32) + got2.astype(F32)
        middle.append((keep, swap(keep[size:].astype(BF), "x", (3, 1)[i % 2])))
    parts = []
    for i, (keep, got3) in enumerate(middle):
        if i < 2:
            got3 = after(got3, started[2][0], started[3][0])
        parts.append(keep[:size] + got3.astype(F32))
    return finish(parts, jnp.concatenate(tables).astype(jnp.int32))


def solution(mesh):
    finer = Mesh(mesh.devices.reshape(4, 4, 4, 2), ("z", "y", "x", "c"))
    in_specs = (P(SEQ, None), P(SEQ, HEAD), P(SEQ, HEAD), P(SEQ, HEAD), P(SEQ, HEAD))
    out_specs = P(SEQ + HEAD, None)
    return jax.shard_map(on_device, mesh=finer, in_specs=in_specs, out_specs=out_specs, check_vma=False)
```

```python
import functools

import jax
import jax.numpy as jnp
from jax import lax
from jax.experimental import pallas as pl
from jax.experimental.pallas import tpu as pltpu
from jax.sharding import Mesh
from jax.sharding import PartitionSpec as P

DH = 128
SEQ = ("z", "y")
HEAD = ("x", "c")
NORM_EPS = 1e-05
STEP_EPS = 1e-06
BF = jnp.bfloat16
F32 = jnp.float32
ORDERS = (
    ((("z", 1), ("z", 3), ("y", 1), ("y", 3)), (("z", 3), ("z", 1), ("y", 3), ("y", 1))),
    ((("y", 1), ("y", 3), ("z", 1), ("z", 3)), (("y", 3), ("y", 1), ("z", 3), ("z", 1))),
)
PARTS = ((0, 8), (8, 12), (12, 16))
NT = (((1,), (1,)), ((), ()))
TN = (((0,), (0,)), ((), ()))


def swap(x, axis, offset):
    n = lax.axis_size(axis)
    return lax.ppermute(x, axis, [(i, i ^ offset) for i in range(n)])


def swap_links(x, half, step):
    pairs = []
    for z in range(4):
        for y in range(4):
            for c in range(2):
                axis, o = ORDERS[half][c][step]
                to_z, to_y = (z ^ o, y) if axis == "z" else (z, y ^ o)
                pairs.append(((z * 4 + y) * 2 + c, (to_z * 4 + to_y) * 2 + c))
    return lax.ppermute(x, ("z", "y", "c"), pairs)


def slot_offsets(half, core):
    inner, outer = ORDERS[half][0][0][0], ORDERS[half][0][2][0]
    slots = []
    for group in (0, 1, 3, 2) if core == 0 else (0, 3, 1, 2):
        for o in (0, 1, 3, 2):
            offset = {inner: o, outer: group}
            slots.append((offset["z"], offset["y"]))
    return slots


def sources(half, core):
    z, y = lax.axis_index("z"), lax.axis_index("y")
    return jnp.stack([((z ^ dz) * 4 + (y ^ dy)) * 2 + half for dz, dy in slot_offsets(half, core)])


def own_sources():
    c = lax.axis_index("c")
    return jnp.stack([jnp.where(c == 0, sources(h, 0), sources(h, 1)) for h in (0, 1)]).astype(jnp.int32)


def after(x, *others):
    return lax.optimization_barrier((x, *others))[0]


def join(held, got, step):
    if step != 1:
        return jnp.concatenate([held, got], axis=0)
    n = 1
    first = lax.axis_index("c") == 0
    inner = [jnp.where(first, held[n:], got[:n]), jnp.where(first, got[:n], held[n:])]
    return jnp.concatenate([held[:n], *inner, got[n:]], axis=0)


def gather(block, ready):
    held = [block[:1], block[1:]]
    for step in (0, 1):
        got = [swap_links(held[h], h, step) for h in (0, 1)]
        held = [join(held[h], got[h], step) for h in (0, 1)]
    near = [swap_links(held[h], h, 2) for h in (0, 1)]
    far = [swap_links(after(held[h], *ready), h, 3) for h in (0, 1)]
    wide = 2 * block.shape[1] // 3
    last_kv = [swap_links(near[h][:, :wide], h, 3) for h in (0, 1)]
    last_q = [swap_links(near[h][:, wide:], h, 3) for h in (0, 1)]
    return held, near, far, last_kv, last_q


def reorder_kernel(table, a, b, *outs):
    k = pl.program_id(0)
    for h, src in enumerate((a, b)):
        turned = src[...].T
        for p, (lo, hi) in enumerate(PARTS):

            @pl.when((k >= lo) & (k < hi))
            def _(out=outs[3 * h + p], turned=turned):
                out[0] = turned


def reorder_columns(hidden, table):
    rows, width = hidden.shape
    q = width // 32
    take = lambda h: pl.BlockSpec((rows, q), lambda k, t, h=h: (0, t[h, k]))
    give = [
        pl.BlockSpec((1, q, rows), lambda k, t, lo=lo, n=hi - lo: (jnp.clip(k - lo, 0, n - 1), 0, 0)) for lo, hi in PARTS
    ]
    return pl.pallas_call(
        reorder_kernel,
        grid_spec=pltpu.PrefetchScalarGridSpec(
            num_scalar_prefetch=1, grid=(16,), in_specs=[take(0), take(1)], out_specs=give * 2
        ),
        out_shape=[jax.ShapeDtypeStruct((hi - lo, q, rows), hidden.dtype) for lo, hi in PARTS] * 2,
        cost_estimate=pl.CostEstimate(flops=0, bytes_accessed=4 * rows * width, transcendentals=0),
        compiler_params=pltpu.CompilerParams(vmem_limit_bytes=2 << 20),
        name="reorder_columns",
    )(table, hidden, hidden)


def finish_kernel(table, a, b, c, d, out):
    parts = (a, b, c, d)
    total = sum(jnp.sum(jnp.square(p[...].astype(F32)), axis=-1, keepdims=True) for p in parts)
    factor = lax.rsqrt(total / out.shape[1] + STEP_EPS)
    for v, p in enumerate(parts):
        for k in range(8):
            cols = pl.ds(pl.multiple_of(table[v * 8 + k] * 256, 256), 256)
            out[:, cols] = jnp.tanh(p[:, k * 256 : (k + 1) * 256].astype(F32) * factor)


def finish(parts, table):
    rows = parts[0].shape[0]
    width = 4 * parts[0].shape[1]
    return pl.pallas_call(
        finish_kernel,
        in_specs=[pl.BlockSpec(memory_space=pltpu.SMEM)] + [pl.BlockSpec(memory_space=pltpu.VMEM)] * 4,
        out_specs=pl.BlockSpec(memory_space=pltpu.VMEM),
        out_shape=jax.ShapeDtypeStruct((rows, width), F32),
        compiler_params=pltpu.CompilerParams(vmem_limit_bytes=10 << 20),
        name="finish",
    )(table, *parts)


def state_round(own, axis, reverse):
    here = lax.axis_index(axis)
    sent = own.astype(BF)
    inside = jnp.zeros_like(own)
    total = own
    for o in (1, 3, 2):
        other = swap(sent, axis, o).astype(F32)
        there = here ^ o
        inside = inside + jnp.where(there > here if reverse else there < here, other, 0.0)
        total = total + other
    return inside, total


def sigmoid(a):
    return 1.0 / (1.0 + jnp.exp(-a))


def silu_slope(preact):
    gate = sigmoid(preact)
    return gate * (1.0 + preact * (1.0 - gate))


def dot(a, b, dims=(((1,), (0,)), ((), ()))):
    return lax.dot_general(a, b, dims, preferred_element_type=F32)


def causal_mask(n):
    return lax.broadcasted_iota(jnp.int32, (n, n), 0) <= lax.broadcasted_iota(jnp.int32, (n, n), 1)


def side_by_side(w):
    return jnp.concatenate([w[k] for k in range(w.shape[0])], axis=1)


def project_kernel(slots, starts, heads, *refs):
    count = len(slots)
    begins, refs = refs[:starts], refs[starts:]
    weights, hids, outs = refs[:count], refs[count : count + 2], refs[count + 2 : -3]
    buf, hid_buf, sems = refs[-3:]
    copies = []
    for i, (half, slot) in enumerate(slots):
        copies.append(pltpu.make_async_copy(weights[i], buf.at[i], sems.at[i]))
        copies.append(pltpu.make_async_copy(hids[half].at[pl.ds(slot, 4)], hid_buf.at[i], sems.at[count + i]))
    for copy in copies:
        copy.start()
    sums = outs[:-1] if heads else outs
    for i in range(count):
        copies[2 * i].wait()
        copies[2 * i + 1].wait()
        t = dot(side_by_side(buf[i]), hid_buf[i].reshape(-1, hid_buf.shape[3]))
        at = 0
        for j, out in enumerate(sums):
            part = t[at : at + out.shape[0]]
            at += out.shape[0]
            if i:
                out[...] += part
            else:
                out[...] = begins[j][...] + part if starts else part

    for h in range(heads):
        out = outs[0]
        pk = out[h * DH : (h + 1) * DH, :]
        k = (pk * sigmoid(pk)).astype(BF)
        v = out[(heads + h) * DH : (heads + h + 1) * DH, :].astype(BF)
        outs[-1][h] = dot(k, v, NT)


def project(limit, weights, slots, hid, widths, start=(), heads=0):
    cols, q = weights[0].shape[1:]
    n = hid[0].shape[2]
    vmem = pl.BlockSpec(memory_space=pltpu.VMEM)
    anywhere = pl.BlockSpec(memory_space=pltpu.HBM)
    out_shape = [jax.ShapeDtypeStruct((w, n), F32) for w in widths]
    if heads:
        out_shape.append(jax.ShapeDtypeStruct((heads, DH, DH), F32))
    count = len(slots)
    return pl.pallas_call(
        functools.partial(project_kernel, slots, len(start), heads),
        in_specs=[vmem] * len(start) + [anywhere] * (count + 2),
        out_specs=[vmem] * len(out_shape),
        out_shape=out_shape,
        scratch_shapes=[
            pltpu.VMEM((count, 4, cols, q), BF),
            pltpu.VMEM((count, 4, q, n), BF),
            pltpu.SemaphoreType.DMA((2 * count,)),
        ],
        cost_estimate=pl.CostEstimate(
            flops=8 * count * cols * q * n, bytes_accessed=8 * count * cols * q, transcendentals=0
        ),
        compiler_params=pltpu.CompilerParams(vmem_limit_bytes=limit << 20),
        name="project",
    )(*start, *weights, *hid)


def attend_kernel(pre_q, pre_k, pre_v, before, cot, own_grad, grad_att):
    pq = pre_q[...]
    pk = pre_k[...]
    q = (pq * sigmoid(pq)).astype(BF)
    k = (pk * sigmoid(pk)).astype(BF)
    v = pre_v[...].astype(BF)
    b = before[0].astype(BF)
    scores = jnp.where(causal_mask(q.shape[1]), dot(k, q, TN), 0.0).astype(BF)
    attended = dot(v, scores) + dot(b, q, TN)
    scale = lax.rsqrt(jnp.mean(attended * attended, axis=0, keepdims=True) + NORM_EPS)
    normed = attended * scale
    up = cot[...].T.astype(F32)
    ga = (scale * (up - normed * jnp.mean(up * normed, axis=0, keepdims=True))).astype(BF)
    grad_att[...] = ga
    own_grad[0] = dot(q, ga, NT)


def attend_back_kernel(pre_q, pre_k, pre_v, before, grad_att, back_q, grad_k, grad_v):
    pq = pre_q[...]
    pk = pre_k[...]
    q = (pq * sigmoid(pq)).astype(BF)
    k = (pk * sigmoid(pk)).astype(BF)
    v = pre_v[...].astype(BF)
    b = before[0].astype(BF)
    ga = grad_att[...]
    causal = causal_mask(q.shape[1])
    scores = jnp.where(causal, dot(k, q, TN), 0.0).astype(BF)
    gs = jnp.where(causal, dot(v, ga, TN), 0.0).astype(BF)
    gq = dot(k, gs) + dot(b, ga)
    back_q[...] = (gq * silu_slope(pq)).astype(BF)
    grad_k[...] = dot(q, gs, NT)
    grad_v[...] = dot(ga, scores, NT)


def head_specs(n, heads):
    row = pl.BlockSpec((DH, n), lambda h: (h, 0))
    row_v = pl.BlockSpec((DH, n), lambda h: (heads + h, 0))
    state = pl.BlockSpec((1, DH, DH), lambda h: (h, 0, 0))
    return row, row_v, state


def attend(pre_query, pre_kv, before, cotangent):
    width, n = pre_query.shape
    heads = width // DH
    row, row_v, state = head_specs(n, heads)
    return pl.pallas_call(
        attend_kernel,
        grid=(heads,),
        in_specs=[row, row, row_v, state, pl.BlockSpec((n, DH), lambda h: (0, h))],
        out_specs=[state, row],
        out_shape=[
            jax.ShapeDtypeStruct((heads, DH, DH), F32),
            jax.ShapeDtypeStruct((width, n), BF),
        ],
        compiler_params=pltpu.CompilerParams(vmem_limit_bytes=4 << 20),
        name="attend",
    )(pre_query, pre_kv, pre_kv, before, cotangent)


def attend_back(pre_query, pre_kv, before, grad_att):
    width, n = pre_query.shape
    heads = width // DH
    row, row_v, state = head_specs(n, heads)
    return pl.pallas_call(
        attend_back_kernel,
        grid=(heads,),
        in_specs=[row, row, row_v, state, row],
        out_specs=[row, row, row],
        out_shape=[
            jax.ShapeDtypeStruct((width, n), BF),
            jax.ShapeDtypeStruct((width, n), F32),
            jax.ShapeDtypeStruct((width, n), F32),
        ],
        cost_estimate=pl.CostEstimate(flops=6 * heads * n * n * DH, bytes_accessed=16 * n * width, transcendentals=0),
        compiler_params=pltpu.CompilerParams(vmem_limit_bytes=4 << 20),
        name="attend_back",
    )(pre_query, pre_kv, pre_kv, before, grad_att)


def row_table():
    x, c = lax.axis_index("x"), lax.axis_index("c")
    groups = []
    for oc in (1, 0):
        owner = c ^ oc
        for ox0, ox1 in ((0, 0), (3, 1), (1, 3), (2, 2)):
            groups.append((x ^ jnp.where(owner == 0, ox0, ox1)) * 2 + owner)
    return jnp.stack(groups).astype(jnp.int32)


def swap_rings(a, step):
    pairs = []
    for x in range(4):
        for c in range(2):
            pairs.append((x * 2 + c, (x ^ ((1, 3), (3, 1))[step][c]) * 2 + c))
    return lax.ppermute(a, ("x", "c"), pairs)


def chunk_copies(kind, srcs, bufs, sems):
    sides = [[(srcs[0], bufs[0])], [(src, buf) for src, buf in zip(srcs[1:], bufs[1:])]]
    pairs = []
    for i in range(4):
        at = pl.ds(2 * (i % 2), 2)
        pairs.append([pltpu.make_async_copy(s.at[at], b.at[at], sems.at[2 * i + j]) for j, (s, b) in enumerate(sides[i // 2])])
    return sides, pairs


def push_chunk(kind, rows, sides, pairs, outs, out_bufs, out_sems):
    half = rows.shape[0] // 2
    c = lax.axis_index("c")
    places = (c, 1 - c) if kind else (0, 1)
    leaving = []
    for i in range(4):
        for copy in pairs[i]:
            copy.wait()
        total, at = None, 0
        for _, buf in sides[i // 2]:
            side = jnp.concatenate([buf[2 * (i % 2)], buf[2 * (i % 2) + 1]], axis=1)
            term = dot(rows[:, at : at + side.shape[0]], side)
            total = term if total is None else total + term
            at += side.shape[0]
        cols = pl.ds(pl.multiple_of(places[i // 2] * 1024 + (i % 2) * 512, 512), 512)
        for j, part in enumerate((total[:half], total[half:])):
            out_bufs[j][i] = part.astype(out_bufs[j].dtype)
            leaving.append(pltpu.make_async_copy(out_bufs[j].at[i], outs[j].at[:, cols], out_sems.at[2 * i + j]))
            leaving[-1].start()
    return leaving


def collect_kernel(count, table, pre_kv, grad_k, grad_v, back_q, later, *refs):
    srcs, (rows_out, other, mine) = refs[:count], refs[count : count + 3]
    back = refs[count + 3]
    bufs = refs[count + 4 : 2 * count + 4]
    other_buf, mine_buf, sems, out_sems, rows, rows_sem = refs[2 * count + 4 :]
    sides, pairs = chunk_copies(0, srcs, bufs, sems)
    for pair in pairs:
        for copy in pair:
            copy.start()
    width, n = back_q.shape
    for h in range(width // DH):
        cols = slice(h * DH, (h + 1) * DH)
        vcols = slice(width + h * DH, width + (h + 1) * DH)
        qcols = slice(2 * width + h * DH, 2 * width + (h + 1) * DH)
        pk = pre_kv[cols, :]
        k = (pk * sigmoid(pk)).astype(BF)
        v = pre_kv[vcols, :].astype(BF)
        a = later[h].astype(BF)
        back[:, cols] = ((grad_k[cols, :] + dot(a, v)) * silu_slope(pk)).astype(BF).T
        back[:, vcols] = (grad_v[cols, :] + dot(a, k, TN)).astype(BF).T
        back[:, qcols] = back_q[cols, :].T
    g = n // 8
    for k in range(8):
        rows[k * g : (k + 1) * g, :] = back[pl.ds(pl.multiple_of(table[k] * g, g), g), :]
    leaving = [pltpu.make_async_copy(rows, rows_out, rows_sem)]
    leaving[0].start()
    leaving += push_chunk(0, rows, sides, pairs, (other, mine), (other_buf, mine_buf), out_sems)
    for copy in leaving:
        copy.wait()


def out_scratch(n):
    return [
        pltpu.VMEM((4, n // 2, 512), BF),
        pltpu.VMEM((4, n // 2, 512), BF),
        pltpu.SemaphoreType.DMA((8,)),
        pltpu.SemaphoreType.DMA((8,)),
    ]


def collect(pre_kv, grad_k, grad_v, back_q, later, weights):
    width, n = back_q.shape
    vmem = pl.BlockSpec(memory_space=pltpu.VMEM)
    hbm = pl.BlockSpec(memory_space=pltpu.HBM)
    return pl.pallas_call(
        functools.partial(collect_kernel, len(weights)),
        in_specs=[pl.BlockSpec(memory_space=pltpu.SMEM)] + [vmem] * 5 + [hbm] * len(weights),
        out_specs=[hbm] * 3,
        out_shape=[jax.ShapeDtypeStruct((n, 3 * width), BF)] + [jax.ShapeDtypeStruct((n // 2, 2048), BF)] * 2,
        scratch_shapes=[
            pltpu.VMEM((n, 3 * width), BF),
            *(pltpu.VMEM(w.shape, BF) for w in weights),
            *out_scratch(n),
            pltpu.VMEM((n, 3 * width), BF),
            pltpu.SemaphoreType.DMA,
        ],
        cost_estimate=pl.CostEstimate(flops=2 * n * 1536 * 2048, bytes_accessed=1536 * 4096, transcendentals=0),
        compiler_params=pltpu.CompilerParams(vmem_limit_bytes=30 << 20),
        name="collect",
    )(row_table(), pre_kv, grad_k, grad_v, back_q, later, *weights)


def push_kernel(kinds, counts, *refs):
    rows_in, srcs = refs[: len(kinds)], refs[len(kinds) : len(kinds) + sum(counts)]
    refs = refs[len(kinds) + sum(counts) :]
    outs, refs = refs[: 2 * len(kinds)], refs[2 * len(kinds) :]
    work = []
    for m, kind in enumerate(kinds):
        at = sum(counts[:m])
        rows, refs = refs[0], refs[1:]
        bufs, refs = refs[: counts[m]], refs[counts[m] :]
        (other_buf, mine_buf, sems, out_sems, rows_sem), refs = refs[:5], refs[5:]
        take_rows = pltpu.make_async_copy(rows_in[m], rows, rows_sem)
        take_rows.start()
        sides, pairs = chunk_copies(kind, srcs[at : at + counts[m]], bufs, sems)
        for pair in pairs:
            for copy in pair:
                copy.start()
        work.append((take_rows, kind, rows, sides, pairs, outs[2 * m : 2 * m + 2], (other_buf, mine_buf), out_sems))
    leaving = []
    for take_rows, *rest in work:
        take_rows.wait()
        leaving += push_chunk(*rest)
    for copy in leaving:
        copy.wait()


def push(share, kinds, rows, weights):
    n = rows[0].shape[0]
    hbm = pl.BlockSpec(memory_space=pltpu.HBM)
    loads = [2 * n * 1536 * 2048 // 100 * share for _ in kinds]
    counts = tuple(map(len, weights))
    scratch = []
    for r, ws in zip(rows, weights):
        scratch += [pltpu.VMEM(r.shape, BF), *(pltpu.VMEM(w.shape, BF) for w in ws), *out_scratch(n), pltpu.SemaphoreType.DMA]
    return pl.pallas_call(
        functools.partial(push_kernel, kinds, counts),
        in_specs=[hbm] * (len(kinds) + sum(counts)),
        out_specs=[hbm] * (2 * len(kinds)),
        out_shape=[jax.ShapeDtypeStruct((n // 2, 2048), BF)] * (2 * len(kinds)),
        scratch_shapes=scratch,
        cost_estimate=pl.CostEstimate(
            flops=int(sum(loads)), bytes_accessed=1, transcendentals=0
        ),
        compiler_params=pltpu.CompilerParams(vmem_limit_bytes=54 << 20),
        name="push",
    )(*rows, *(w for ws in weights for w in ws))


def transposed(w):
    return jnp.swapaxes(w.reshape(2, w.shape[0] // 2, w.shape[1]), 1, 2)


def on_device(hidden, w_query, w_key, w_value, cotangent):
    heads = w_query.shape[1] // DH
    n = hidden.shape[0]
    hid = reorder_columns(hidden, own_sources())
    block = jnp.concatenate([transposed(w_key), transposed(w_value), transposed(w_query)], axis=1)
    held, near, far, last_kv, last_q = gather(block, hid)
    wide = 2 * heads * DH
    sums = project(20, [held[0], near[0], held[1], near[1]], ((0, 0), (0, 4), (1, 0), (1, 4)), hid[0::3], (wide, wide // 2))
    sums = project(14, far, ((0, 0), (1, 0)), hid[1::3], (wide, wide // 2), sums)
    pre_kv, own_state = project(44, last_kv, ((0, 0), (1, 0)), hid[2::3], (wide,), sums[:1], heads)
    inner, total = state_round(own_state, "y", False)
    outer, _ = state_round(total, "z", False)
    before = inner + outer
    pre_query = project(44, last_q, ((0, 0), (1, 0)), hid[2::3], (wide // 2,), sums[1:])[0]
    own_grad, grad_att = attend(pre_query, pre_kv, before, cotangent)
    back_q, grad_k, grad_v = attend_back(pre_query, pre_kv, before, grad_att)
    inner, total = state_round(own_grad, "y", True)
    outer, _ = state_round(after(total, back_q), "z", True)
    later = inner + outer
    weights = [w for h in (0, 1) for w in ((held[h], last_kv[h], last_q[h]), (near[h], far[h]))]
    rows, *chunk = collect(pre_kv, grad_k, grad_v, back_q, later, weights[0])
    size = n // 8
    started = []
    for i in range(4):
        if i:
            use = rows
            if i == 2:
                use = after(rows, started[0][0])
            if i == 3:
                use = after(rows, started[1][0], started[0][1][0])
            chunk = push(100, (i % 2,), (use,), weights[i : i + 1])
        other, mine = chunk
        got = swap(other, "c", 1)
        send = (mine[2 * size :].astype(F32) + got[2 * size :].astype(F32)).astype(BF)
        got = mine[: 2 * size].astype(F32) + got[: 2 * size].astype(F32)
        got2 = swap_rings(send, 0)
        keep = got + got2.astype(F32)
        started.append((send, (got2, keep[size:].astype(BF)), keep))
    tables = []
    for h in (0, 1):
        src = sources(h, 0)
        for picks in ((0, 1, 2, 3, 12, 13, 14, 15), (4, 5, 6, 7, 8, 9, 10, 11)):
            tables.append(jnp.stack([src[p] for p in picks]))
    parts = []
    for i, (_, (_, send), keep) in enumerate(started):
        got = swap_rings(send, 1)
        if i < 2:
            got = after(got, started[2][0], started[3][0])
        parts.append(keep[:size] + got.astype(F32))
    return finish(parts, jnp.concatenate(tables).astype(jnp.int32))


def solution(mesh):
    finer = Mesh(mesh.devices.reshape(4, 4, 4, 2), ("z", "y", "x", "c"))
    in_specs = (P(SEQ, None), P(SEQ, HEAD), P(SEQ, HEAD), P(SEQ, HEAD), P(SEQ, HEAD))
    out_specs = P(SEQ + HEAD, None)
    return jax.shard_map(on_device, mesh=finer, in_specs=in_specs, out_specs=out_specs, check_vma=False)
```

```python
import functools

import jax
import jax.numpy as jnp
from jax import lax
from jax.experimental import pallas as pl
from jax.experimental.pallas import tpu as pltpu
from jax.sharding import Mesh
from jax.sharding import PartitionSpec as P

DH = 128
SEQ = ("z", "y")
HEAD = ("x", "c")
NORM_EPS = 1e-05
STEP_EPS = 1e-06
BF = jnp.bfloat16
F32 = jnp.float32
ORDERS = (
    ((("z", 1), ("z", 3), ("y", 1), ("y", 3)), (("z", 3), ("z", 1), ("y", 3), ("y", 1))),
    ((("y", 1), ("y", 3), ("z", 1), ("z", 3)), (("y", 3), ("y", 1), ("z", 3), ("z", 1))),
)
PARTS = ((0, 8), (8, 12), (12, 16))
NT = (((1,), (1,)), ((), ()))
TN = (((0,), (0,)), ((), ()))


def swap(x, axis, offset):
    n = lax.axis_size(axis)
    return lax.ppermute(x, axis, [(i, i ^ offset) for i in range(n)])


def swap_links(x, half, step):
    pairs = []
    for z in range(4):
        for y in range(4):
            for c in range(2):
                axis, o = ORDERS[half][c][step]
                to_z, to_y = (z ^ o, y) if axis == "z" else (z, y ^ o)
                pairs.append(((z * 4 + y) * 2 + c, (to_z * 4 + to_y) * 2 + c))
    return lax.ppermute(x, ("z", "y", "c"), pairs)


def slot_offsets(half, core):
    inner, outer = ORDERS[half][0][0][0], ORDERS[half][0][2][0]
    slots = []
    for group in (0, 1, 3, 2) if core == 0 else (0, 3, 1, 2):
        for o in (0, 1, 3, 2):
            offset = {inner: o, outer: group}
            slots.append((offset["z"], offset["y"]))
    return slots


def sources(half, core):
    z, y = lax.axis_index("z"), lax.axis_index("y")
    return jnp.stack([((z ^ dz) * 4 + (y ^ dy)) * 2 + half for dz, dy in slot_offsets(half, core)])


def own_sources():
    c = lax.axis_index("c")
    return jnp.stack([jnp.where(c == 0, sources(h, 0), sources(h, 1)) for h in (0, 1)]).astype(jnp.int32)


def after(x, *others):
    return lax.optimization_barrier((x, *others))[0]


def join(held, got, step):
    if step != 1:
        return jnp.concatenate([held, got], axis=0)
    n = 1
    first = lax.axis_index("c") == 0
    inner = [jnp.where(first, held[n:], got[:n]), jnp.where(first, got[:n], held[n:])]
    return jnp.concatenate([held[:n], *inner, got[n:]], axis=0)


def gather(block, ready):
    held = [block[:1], block[1:]]
    for step in (0, 1):
        got = [swap_links(held[h], h, step) for h in (0, 1)]
        held = [join(held[h], got[h], step) for h in (0, 1)]
    near = [swap_links(held[h], h, 2) for h in (0, 1)]
    far = [swap_links(after(held[h], *ready), h, 3) for h in (0, 1)]
    wide = 2 * block.shape[1] // 3
    last_kv = [swap_links(near[h][:, :wide], h, 3) for h in (0, 1)]
    last_q = [swap_links(near[h][:, wide:], h, 3) for h in (0, 1)]
    return held, near, far, last_kv, last_q


def reorder_kernel(table, a, b, *outs):
    k = pl.program_id(0)
    for h, src in enumerate((a, b)):
        turned = src[...].T
        for p, (lo, hi) in enumerate(PARTS):

            @pl.when((k >= lo) & (k < hi))
            def _(out=outs[3 * h + p], turned=turned):
                out[0] = turned


def reorder_columns(hidden, table):
    rows, width = hidden.shape
    q = width // 32
    take = lambda h: pl.BlockSpec((rows, q), lambda k, t, h=h: (0, t[h, k]))
    give = [
        pl.BlockSpec((1, q, rows), lambda k, t, lo=lo, n=hi - lo: (jnp.clip(k - lo, 0, n - 1), 0, 0)) for lo, hi in PARTS
    ]
    return pl.pallas_call(
        reorder_kernel,
        grid_spec=pltpu.PrefetchScalarGridSpec(
            num_scalar_prefetch=1, grid=(16,), in_specs=[take(0), take(1)], out_specs=give * 2
        ),
        out_shape=[jax.ShapeDtypeStruct((hi - lo, q, rows), hidden.dtype) for lo, hi in PARTS] * 2,
        cost_estimate=pl.CostEstimate(flops=0, bytes_accessed=4 * rows * width, transcendentals=0),
        compiler_params=pltpu.CompilerParams(vmem_limit_bytes=2 << 20),
        name="reorder_columns",
    )(table, hidden, hidden)


def finish_kernel(table, a, b, c, d, out):
    parts = (a, b, c, d)
    total = sum(jnp.sum(jnp.square(p[...].astype(F32)), axis=-1, keepdims=True) for p in parts)
    factor = lax.rsqrt(total / out.shape[1] + STEP_EPS)
    for v, p in enumerate(parts):
        for k in range(8):
            cols = pl.ds(pl.multiple_of(table[v * 8 + k] * 256, 256), 256)
            out[:, cols] = jnp.tanh(p[:, k * 256 : (k + 1) * 256].astype(F32) * factor)


def finish(parts, table):
    rows = parts[0].shape[0]
    width = 4 * parts[0].shape[1]
    return pl.pallas_call(
        finish_kernel,
        in_specs=[pl.BlockSpec(memory_space=pltpu.SMEM)] + [pl.BlockSpec(memory_space=pltpu.VMEM)] * 4,
        out_specs=pl.BlockSpec(memory_space=pltpu.VMEM),
        out_shape=jax.ShapeDtypeStruct((rows, width), F32),
        compiler_params=pltpu.CompilerParams(vmem_limit_bytes=10 << 20),
        name="finish",
    )(table, *parts)


def state_round(own, axis, reverse):
    here = lax.axis_index(axis)
    sent = own.astype(BF)
    inside = jnp.zeros_like(own)
    total = own
    for o in (1, 3, 2):
        other = swap(sent, axis, o).astype(F32)
        there = here ^ o
        inside = inside + jnp.where(there > here if reverse else there < here, other, 0.0)
        total = total + other
    return inside, total


def sigmoid(a):
    return 1.0 / (1.0 + jnp.exp(-a))


def silu_slope(preact):
    gate = sigmoid(preact)
    return gate * (1.0 + preact * (1.0 - gate))


def dot(a, b, dims=(((1,), (0,)), ((), ()))):
    return lax.dot_general(a, b, dims, preferred_element_type=F32)


def causal_mask(n):
    return lax.broadcasted_iota(jnp.int32, (n, n), 0) <= lax.broadcasted_iota(jnp.int32, (n, n), 1)


def side_by_side(w):
    return jnp.concatenate([w[k] for k in range(w.shape[0])], axis=1)


def project_kernel(slots, starts, heads, *refs):
    count = len(slots)
    begins, refs = refs[:starts], refs[starts:]
    weights, hids, outs = refs[:count], refs[count : count + 2], refs[count + 2 : -3]
    buf, hid_buf, sems = refs[-3:]
    copies = []
    for i, (half, slot) in enumerate(slots):
        copies.append(pltpu.make_async_copy(weights[i], buf.at[i], sems.at[i]))
        copies.append(pltpu.make_async_copy(hids[half].at[pl.ds(slot, 4)], hid_buf.at[i], sems.at[count + i]))
    for copy in copies:
        copy.start()
    sums = outs[:-1] if heads else outs
    for i in range(count):
        copies[2 * i].wait()
        copies[2 * i + 1].wait()
        t = dot(side_by_side(buf[i]), hid_buf[i].reshape(-1, hid_buf.shape[3]))
        at = 0
        for j, out in enumerate(sums):
            part = t[at : at + out.shape[0]]
            at += out.shape[0]
            if i:
                out[...] += part
            else:
                out[...] = begins[j][...] + part if starts else part

    for h in range(heads):
        out = outs[0]
        pk = out[h * DH : (h + 1) * DH, :]
        k = (pk * sigmoid(pk)).astype(BF)
        v = out[(heads + h) * DH : (heads + h + 1) * DH, :].astype(BF)
        outs[-1][h] = dot(k, v, NT)


def project(limit, weights, slots, hid, widths, start=(), heads=0):
    cols, q = weights[0].shape[1:]
    n = hid[0].shape[2]
    vmem = pl.BlockSpec(memory_space=pltpu.VMEM)
    anywhere = pl.BlockSpec(memory_space=pltpu.HBM)
    out_shape = [jax.ShapeDtypeStruct((w, n), F32) for w in widths]
    if heads:
        out_shape.append(jax.ShapeDtypeStruct((heads, DH, DH), F32))
    count = len(slots)
    return pl.pallas_call(
        functools.partial(project_kernel, slots, len(start), heads),
        in_specs=[vmem] * len(start) + [anywhere] * (count + 2),
        out_specs=[vmem] * len(out_shape),
        out_shape=out_shape,
        scratch_shapes=[
            pltpu.VMEM((count, 4, cols, q), BF),
            pltpu.VMEM((count, 4, q, n), BF),
            pltpu.SemaphoreType.DMA((2 * count,)),
        ],
        cost_estimate=pl.CostEstimate(
            flops=8 * count * cols * q * n, bytes_accessed=8 * count * cols * q, transcendentals=0
        ),
        compiler_params=pltpu.CompilerParams(vmem_limit_bytes=limit << 20),
        name="project",
    )(*start, *weights, *hid)


def attend_kernel(pre_q, pre_k, pre_v, before, cot, own_grad, grad_att):
    pq = pre_q[...]
    pk = pre_k[...]
    q = (pq * sigmoid(pq)).astype(BF)
    k = (pk * sigmoid(pk)).astype(BF)
    v = pre_v[...].astype(BF)
    b = before[0].astype(BF)
    scores = jnp.where(causal_mask(q.shape[1]), dot(k, q, TN), 0.0).astype(BF)
    attended = dot(v, scores) + dot(b, q, TN)
    scale = lax.rsqrt(jnp.mean(attended * attended, axis=0, keepdims=True) + NORM_EPS)
    normed = attended * scale
    up = cot[...].T.astype(F32)
    ga = (scale * (up - normed * jnp.mean(up * normed, axis=0, keepdims=True))).astype(BF)
    grad_att[...] = ga
    own_grad[0] = dot(q, ga, NT)


def attend_back_kernel(pre_q, pre_k, pre_v, before, grad_att, back_q, grad_k, grad_v):
    pq = pre_q[...]
    pk = pre_k[...]
    q = (pq * sigmoid(pq)).astype(BF)
    k = (pk * sigmoid(pk)).astype(BF)
    v = pre_v[...].astype(BF)
    b = before[0].astype(BF)
    ga = grad_att[...]
    causal = causal_mask(q.shape[1])
    scores = jnp.where(causal, dot(k, q, TN), 0.0).astype(BF)
    gs = jnp.where(causal, dot(v, ga, TN), 0.0).astype(BF)
    gq = dot(k, gs) + dot(b, ga)
    back_q[...] = (gq * silu_slope(pq)).astype(BF)
    grad_k[...] = dot(q, gs, NT)
    grad_v[...] = dot(ga, scores, NT)


def head_specs(n, heads):
    row = pl.BlockSpec((DH, n), lambda h: (h, 0))
    row_v = pl.BlockSpec((DH, n), lambda h: (heads + h, 0))
    state = pl.BlockSpec((1, DH, DH), lambda h: (h, 0, 0))
    return row, row_v, state


def attend(pre_query, pre_kv, before, cotangent):
    width, n = pre_query.shape
    heads = width // DH
    row, row_v, state = head_specs(n, heads)
    return pl.pallas_call(
        attend_kernel,
        grid=(heads,),
        in_specs=[row, row, row_v, state, pl.BlockSpec((n, DH), lambda h: (0, h))],
        out_specs=[state, row],
        out_shape=[
            jax.ShapeDtypeStruct((heads, DH, DH), F32),
            jax.ShapeDtypeStruct((width, n), BF),
        ],
        compiler_params=pltpu.CompilerParams(vmem_limit_bytes=4 << 20),
        name="attend",
    )(pre_query, pre_kv, pre_kv, before, cotangent)


def attend_back(pre_query, pre_kv, before, grad_att):
    width, n = pre_query.shape
    heads = width // DH
    row, row_v, state = head_specs(n, heads)
    return pl.pallas_call(
        attend_back_kernel,
        grid=(heads,),
        in_specs=[row, row, row_v, state, row],
        out_specs=[row, row, row],
        out_shape=[
            jax.ShapeDtypeStruct((width, n), BF),
            jax.ShapeDtypeStruct((width, n), F32),
            jax.ShapeDtypeStruct((width, n), F32),
        ],
        cost_estimate=pl.CostEstimate(flops=6 * heads * n * n * DH, bytes_accessed=16 * n * width, transcendentals=0),
        compiler_params=pltpu.CompilerParams(vmem_limit_bytes=4 << 20),
        name="attend_back",
    )(pre_query, pre_kv, pre_kv, before, grad_att)


def row_table():
    x, c = lax.axis_index("x"), lax.axis_index("c")
    groups = []
    for oc in (1, 0):
        owner = c ^ oc
        for ox0, ox1 in ((0, 0), (3, 1), (1, 3), (2, 2)):
            groups.append((x ^ jnp.where(owner == 0, ox0, ox1)) * 2 + owner)
    return jnp.stack(groups).astype(jnp.int32)


def swap_rings(a, step):
    pairs = []
    for x in range(4):
        for c in range(2):
            pairs.append((x * 2 + c, (x ^ ((1, 3), (3, 1))[step][c]) * 2 + c))
    return lax.ppermute(a, ("x", "c"), pairs)


def chunk_copies(kind, srcs, bufs, sems):
    sides = [[(srcs[0], bufs[0])], [(src, buf) for src, buf in zip(srcs[1:], bufs[1:])]]
    pairs = []
    for i in range(4):
        at = pl.ds(2 * (i % 2), 2)
        pairs.append([pltpu.make_async_copy(s.at[at], b.at[at], sems.at[2 * i + j]) for j, (s, b) in enumerate(sides[i // 2])])
    return sides, pairs


def push_chunk(kind, rows, sides, pairs, outs, out_bufs, out_sems):
    half = rows.shape[0] // 2
    c = lax.axis_index("c")
    places = (c, 1 - c) if kind else (0, 1)
    leaving = []
    for i in range(4):
        for copy in pairs[i]:
            copy.wait()
        total, at = None, 0
        for _, buf in sides[i // 2]:
            side = jnp.concatenate([buf[2 * (i % 2)], buf[2 * (i % 2) + 1]], axis=1)
            term = dot(rows[:, at : at + side.shape[0]], side)
            total = term if total is None else total + term
            at += side.shape[0]
        cols = pl.ds(pl.multiple_of(places[i // 2] * 1024 + (i % 2) * 512, 512), 512)
        for j, part in enumerate((total[:half], total[half:])):
            out_bufs[j][i] = part.astype(out_bufs[j].dtype)
            leaving.append(pltpu.make_async_copy(out_bufs[j].at[i], outs[j].at[:, cols], out_sems.at[2 * i + j]))
            leaving[-1].start()
    return leaving


def collect_kernel(count, table, pre_kv, grad_k, grad_v, back_q, later, *refs):
    srcs, (rows_out, other, mine) = refs[:count], refs[count : count + 3]
    back = refs[count + 3]
    bufs = refs[count + 4 : 2 * count + 4]
    other_buf, mine_buf, sems, out_sems, rows, rows_sem = refs[2 * count + 4 :]
    sides, pairs = chunk_copies(0, srcs, bufs, sems)
    for pair in pairs:
        for copy in pair:
            copy.start()
    width, n = back_q.shape
    for h in range(width // DH):
        cols = slice(h * DH, (h + 1) * DH)
        vcols = slice(width + h * DH, width + (h + 1) * DH)
        qcols = slice(2 * width + h * DH, 2 * width + (h + 1) * DH)
        pk = pre_kv[cols, :]
        k = (pk * sigmoid(pk)).astype(BF)
        v = pre_kv[vcols, :].astype(BF)
        a = later[h].astype(BF)
        back[:, cols] = ((grad_k[cols, :] + dot(a, v)) * silu_slope(pk)).astype(BF).T
        back[:, vcols] = (grad_v[cols, :] + dot(a, k, TN)).astype(BF).T
        back[:, qcols] = back_q[cols, :].T
    g = n // 8
    for k in range(8):
        rows[k * g : (k + 1) * g, :] = back[pl.ds(pl.multiple_of(table[k] * g, g), g), :]
    leaving = [pltpu.make_async_copy(rows, rows_out, rows_sem)]
    leaving[0].start()
    leaving += push_chunk(0, rows, sides, pairs, (other, mine), (other_buf, mine_buf), out_sems)
    for copy in leaving:
        copy.wait()


def out_scratch(n):
    return [
        pltpu.VMEM((4, n // 2, 512), BF),
        pltpu.VMEM((4, n // 2, 512), BF),
        pltpu.SemaphoreType.DMA((8,)),
        pltpu.SemaphoreType.DMA((8,)),
    ]


def collect(pre_kv, grad_k, grad_v, back_q, later, weights):
    width, n = back_q.shape
    vmem = pl.BlockSpec(memory_space=pltpu.VMEM)
    hbm = pl.BlockSpec(memory_space=pltpu.HBM)
    return pl.pallas_call(
        functools.partial(collect_kernel, len(weights)),
        in_specs=[pl.BlockSpec(memory_space=pltpu.SMEM)] + [vmem] * 5 + [hbm] * len(weights),
        out_specs=[hbm] * 3,
        out_shape=[jax.ShapeDtypeStruct((n, 3 * width), BF)] + [jax.ShapeDtypeStruct((n // 2, 2048), BF)] * 2,
        scratch_shapes=[
            pltpu.VMEM((n, 3 * width), BF),
            *(pltpu.VMEM(w.shape, BF) for w in weights),
            *out_scratch(n),
            pltpu.VMEM((n, 3 * width), BF),
            pltpu.SemaphoreType.DMA,
        ],
        cost_estimate=pl.CostEstimate(flops=2 * n * 1536 * 2048, bytes_accessed=1536 * 4096, transcendentals=0),
        compiler_params=pltpu.CompilerParams(vmem_limit_bytes=54 << 20),
        name="collect",
    )(row_table(), pre_kv, grad_k, grad_v, back_q, later, *weights)


def push_kernel(kinds, counts, *refs):
    rows_in, srcs = refs[: len(kinds)], refs[len(kinds) : len(kinds) + sum(counts)]
    refs = refs[len(kinds) + sum(counts) :]
    outs, refs = refs[: 2 * len(kinds)], refs[2 * len(kinds) :]
    work = []
    for m, kind in enumerate(kinds):
        at = sum(counts[:m])
        rows, refs = refs[0], refs[1:]
        bufs, refs = refs[: counts[m]], refs[counts[m] :]
        (other_buf, mine_buf, sems, out_sems, rows_sem), refs = refs[:5], refs[5:]
        take_rows = pltpu.make_async_copy(rows_in[m], rows, rows_sem)
        take_rows.start()
        sides, pairs = chunk_copies(kind, srcs[at : at + counts[m]], bufs, sems)
        for pair in pairs:
            for copy in pair:
                copy.start()
        work.append((take_rows, kind, rows, sides, pairs, outs[2 * m : 2 * m + 2], (other_buf, mine_buf), out_sems))
    leaving = []
    for take_rows, *rest in work:
        take_rows.wait()
        leaving += push_chunk(*rest)
    for copy in leaving:
        copy.wait()


def push(share, kinds, rows, weights):
    n = rows[0].shape[0]
    hbm = pl.BlockSpec(memory_space=pltpu.HBM)
    loads = [2 * n * 1536 * 2048 // 100 * share for _ in kinds]
    counts = tuple(map(len, weights))
    scratch = []
    for r, ws in zip(rows, weights):
        scratch += [pltpu.VMEM(r.shape, BF), *(pltpu.VMEM(w.shape, BF) for w in ws), *out_scratch(n), pltpu.SemaphoreType.DMA]
    return pl.pallas_call(
        functools.partial(push_kernel, kinds, counts),
        in_specs=[hbm] * (len(kinds) + sum(counts)),
        out_specs=[hbm] * (2 * len(kinds)),
        out_shape=[jax.ShapeDtypeStruct((n // 2, 2048), BF)] * (2 * len(kinds)),
        scratch_shapes=scratch,
        cost_estimate=pl.CostEstimate(
            flops=int(sum(loads)), bytes_accessed=1, transcendentals=0
        ),
        compiler_params=pltpu.CompilerParams(vmem_limit_bytes=54 << 20),
        name="push",
    )(*rows, *(w for ws in weights for w in ws))


def transposed(w):
    return jnp.swapaxes(w.reshape(2, w.shape[0] // 2, w.shape[1]), 1, 2)


def on_device(hidden, w_query, w_key, w_value, cotangent):
    heads = w_query.shape[1] // DH
    n = hidden.shape[0]
    hid = reorder_columns(hidden, own_sources())
    block = jnp.concatenate([transposed(w_key), transposed(w_value), transposed(w_query)], axis=1)
    held, near, far, last_kv, last_q = gather(block, hid)
    wide = 2 * heads * DH
    sums = project(20, [held[0], near[0], held[1], near[1]], ((0, 0), (0, 4), (1, 0), (1, 4)), hid[0::3], (wide, wide // 2))
    sums = project(14, far, ((0, 0), (1, 0)), hid[1::3], (wide, wide // 2), sums)
    pre_kv, own_state = project(44, last_kv, ((0, 0), (1, 0)), hid[2::3], (wide,), sums[:1], heads)
    inner, total = state_round(own_state, "y", False)
    outer, _ = state_round(total, "z", False)
    before = inner + outer
    pre_query = project(44, last_q, ((0, 0), (1, 0)), hid[2::3], (wide // 2,), sums[1:])[0]
    own_grad, grad_att = attend(pre_query, pre_kv, before, cotangent)
    back_q, grad_k, grad_v = attend_back(pre_query, pre_kv, before, grad_att)
    inner, total = state_round(own_grad, "y", True)
    outer, _ = state_round(after(total, back_q), "z", True)
    later = inner + outer
    weights = [w for h in (0, 1) for w in ((held[h], last_kv[h], last_q[h]), (near[h], far[h]))]
    rows, *chunk = collect(pre_kv, grad_k, grad_v, back_q, later, weights[0])
    size = n // 8
    started = []
    for i in range(4):
        if i:
            use = rows
            if i == 2:
                use = after(rows, started[0][0])
            if i == 3:
                use = after(rows, started[1][0], started[0][1][0])
            chunk = push(100, (i % 2,), (use,), weights[i : i + 1])
        other, mine = chunk
        got = swap(other, "c", 1)
        send = (mine[2 * size :].astype(F32) + got[2 * size :].astype(F32)).astype(BF)
        got = mine[: 2 * size].astype(F32) + got[: 2 * size].astype(F32)
        got2 = swap_rings(send, 0)
        keep = got + got2.astype(F32)
        started.append((send, (got2, keep[size:].astype(BF)), keep))
    tables = []
    for h in (0, 1):
        src = sources(h, 0)
        for picks in ((0, 1, 2, 3, 12, 13, 14, 15), (4, 5, 6, 7, 8, 9, 10, 11)):
            tables.append(jnp.stack([src[p] for p in picks]))
    parts = []
    for i, (_, (_, send), keep) in enumerate(started):
        got = swap_rings(send, 1)
        if i < 2:
            got = after(got, started[2][0], started[3][0])
        parts.append(keep[:size] + got.astype(F32))
    return finish(parts, jnp.concatenate(tables).astype(jnp.int32))


def solution(mesh):
    finer = Mesh(mesh.devices.reshape(4, 4, 4, 2), ("z", "y", "x", "c"))
    in_specs = (P(SEQ, None), P(SEQ, HEAD), P(SEQ, HEAD), P(SEQ, HEAD), P(SEQ, HEAD))
    out_specs = P(SEQ + HEAD, None)
    return jax.shard_map(on_device, mesh=finer, in_specs=in_specs, out_specs=out_specs, check_vma=False)
```

```python
import functools

import jax
import jax.numpy as jnp
from jax import lax
from jax.experimental import pallas as pl
from jax.experimental.pallas import tpu as pltpu
from jax.sharding import Mesh
from jax.sharding import PartitionSpec as P

DH = 128
SEQ = ("z", "y")
HEAD = ("x", "c")
NORM_EPS = 1e-05
STEP_EPS = 1e-06
BF = jnp.bfloat16
F32 = jnp.float32
ORDERS = (
    ((("z", 1), ("z", 3), ("y", 1), ("y", 3)), (("z", 3), ("z", 1), ("y", 3), ("y", 1))),
    ((("y", 1), ("y", 3), ("z", 1), ("z", 3)), (("y", 3), ("y", 1), ("z", 3), ("z", 1))),
)
PARTS = ((0, 8), (8, 12), (12, 16))
NT = (((1,), (1,)), ((), ()))
TN = (((0,), (0,)), ((), ()))


def swap(x, axis, offset):
    n = lax.axis_size(axis)
    return lax.ppermute(x, axis, [(i, i ^ offset) for i in range(n)])


def swap_links(x, half, step):
    pairs = []
    for z in range(4):
        for y in range(4):
            for c in range(2):
                axis, o = ORDERS[half][c][step]
                to_z, to_y = (z ^ o, y) if axis == "z" else (z, y ^ o)
                pairs.append(((z * 4 + y) * 2 + c, (to_z * 4 + to_y) * 2 + c))
    return lax.ppermute(x, ("z", "y", "c"), pairs)


def slot_offsets(half, core):
    inner, outer = ORDERS[half][0][0][0], ORDERS[half][0][2][0]
    slots = []
    for group in (0, 1, 3, 2) if core == 0 else (0, 3, 1, 2):
        for o in (0, 1, 3, 2):
            offset = {inner: o, outer: group}
            slots.append((offset["z"], offset["y"]))
    return slots


def sources(half, core):
    z, y = lax.axis_index("z"), lax.axis_index("y")
    return jnp.stack([((z ^ dz) * 4 + (y ^ dy)) * 2 + half for dz, dy in slot_offsets(half, core)])


def own_sources():
    c = lax.axis_index("c")
    return jnp.stack([jnp.where(c == 0, sources(h, 0), sources(h, 1)) for h in (0, 1)]).astype(jnp.int32)


def after(x, *others):
    return lax.optimization_barrier((x, *others))[0]


def join(held, got, step):
    if step != 1:
        return jnp.concatenate([held, got], axis=0)
    n = 1
    first = lax.axis_index("c") == 0
    inner = [jnp.where(first, held[n:], got[:n]), jnp.where(first, got[:n], held[n:])]
    return jnp.concatenate([held[:n], *inner, got[n:]], axis=0)


def gather(block, ready):
    held = [block[:1], block[1:]]
    for step in (0, 1):
        got = [swap_links(held[h], h, step) for h in (0, 1)]
        held = [join(held[h], got[h], step) for h in (0, 1)]
    near = [swap_links(held[h], h, 2) for h in (0, 1)]
    far = [swap_links(after(held[h], *ready), h, 3) for h in (0, 1)]
    wide = 2 * block.shape[1] // 3
    last_kv = [swap_links(near[h][:, :wide], h, 3) for h in (0, 1)]
    last_q = [swap_links(near[h][:, wide:], h, 3) for h in (0, 1)]
    return held, near, far, last_kv, last_q


def reorder_kernel(table, a, b, *outs):
    k = pl.program_id(0)
    for h, src in enumerate((a, b)):
        turned = src[...].T
        for p, (lo, hi) in enumerate(PARTS):

            @pl.when((k >= lo) & (k < hi))
            def _(out=outs[3 * h + p], turned=turned):
                out[0] = turned


def reorder_columns(hidden, table):
    rows, width = hidden.shape
    q = width // 32
    take = lambda h: pl.BlockSpec((rows, q), lambda k, t, h=h: (0, t[h, k]))
    give = [
        pl.BlockSpec((1, q, rows), lambda k, t, lo=lo, n=hi - lo: (jnp.clip(k - lo, 0, n - 1), 0, 0)) for lo, hi in PARTS
    ]
    return pl.pallas_call(
        reorder_kernel,
        grid_spec=pltpu.PrefetchScalarGridSpec(
            num_scalar_prefetch=1, grid=(16,), in_specs=[take(0), take(1)], out_specs=give * 2
        ),
        out_shape=[jax.ShapeDtypeStruct((hi - lo, q, rows), hidden.dtype) for lo, hi in PARTS] * 2,
        cost_estimate=pl.CostEstimate(flops=0, bytes_accessed=4 * rows * width, transcendentals=0),
        compiler_params=pltpu.CompilerParams(vmem_limit_bytes=2 << 20),
        name="reorder_columns",
    )(table, hidden, hidden)


def finish_kernel(table, a, b, c, d, out):
    parts = (a, b, c, d)
    total = sum(jnp.sum(jnp.square(p[...].astype(F32)), axis=-1, keepdims=True) for p in parts)
    factor = lax.rsqrt(total / out.shape[1] + STEP_EPS)
    for v, p in enumerate(parts):
        for k in range(8):
            cols = pl.ds(pl.multiple_of(table[v * 8 + k] * 256, 256), 256)
            out[:, cols] = jnp.tanh(p[:, k * 256 : (k + 1) * 256].astype(F32) * factor)


def finish(parts, table):
    rows = parts[0].shape[0]
    width = 4 * parts[0].shape[1]
    return pl.pallas_call(
        finish_kernel,
        in_specs=[pl.BlockSpec(memory_space=pltpu.SMEM)] + [pl.BlockSpec(memory_space=pltpu.VMEM)] * 4,
        out_specs=pl.BlockSpec(memory_space=pltpu.VMEM),
        out_shape=jax.ShapeDtypeStruct((rows, width), F32),
        compiler_params=pltpu.CompilerParams(vmem_limit_bytes=10 << 20),
        name="finish",
    )(table, *parts)


def state_round(own, axis, reverse):
    here = lax.axis_index(axis)
    sent = own.astype(BF)
    inside = jnp.zeros_like(own)
    total = own
    for o in (1, 3, 2):
        other = swap(sent, axis, o).astype(F32)
        there = here ^ o
        inside = inside + jnp.where(there > here if reverse else there < here, other, 0.0)
        total = total + other
    return inside, total


def sigmoid(a):
    return 1.0 / (1.0 + jnp.exp(-a))


def silu_slope(preact):
    gate = sigmoid(preact)
    return gate * (1.0 + preact * (1.0 - gate))


def dot(a, b, dims=(((1,), (0,)), ((), ()))):
    return lax.dot_general(a, b, dims, preferred_element_type=F32)


def causal_mask(n):
    return lax.broadcasted_iota(jnp.int32, (n, n), 0) <= lax.broadcasted_iota(jnp.int32, (n, n), 1)


def side_by_side(w):
    return jnp.concatenate([w[k] for k in range(w.shape[0])], axis=1)


def project_kernel(slots, starts, heads, *refs):
    count = len(slots)
    begins, refs = refs[:starts], refs[starts:]
    weights, hids, outs = refs[:count], refs[count : count + 2], refs[count + 2 : -3]
    buf, hid_buf, sems = refs[-3:]
    copies = []
    for i, (half, slot) in enumerate(slots):
        copies.append(pltpu.make_async_copy(weights[i], buf.at[i], sems.at[i]))
        copies.append(pltpu.make_async_copy(hids[half].at[pl.ds(slot, 4)], hid_buf.at[i], sems.at[count + i]))
    for copy in copies:
        copy.start()
    sums = outs[:-1] if heads else outs
    for i in range(count):
        copies[2 * i].wait()
        copies[2 * i + 1].wait()
        t = dot(side_by_side(buf[i]), hid_buf[i].reshape(-1, hid_buf.shape[3]))
        at = 0
        for j, out in enumerate(sums):
            part = t[at : at + out.shape[0]]
            at += out.shape[0]
            if i:
                out[...] += part
            else:
                out[...] = begins[j][...] + part if starts else part

    for h in range(heads):
        out = outs[0]
        pk = out[h * DH : (h + 1) * DH, :]
        k = (pk * sigmoid(pk)).astype(BF)
        v = out[(heads + h) * DH : (heads + h + 1) * DH, :].astype(BF)
        outs[-1][h] = dot(k, v, NT)


def project(limit, weights, slots, hid, widths, start=(), heads=0):
    cols, q = weights[0].shape[1:]
    n = hid[0].shape[2]
    vmem = pl.BlockSpec(memory_space=pltpu.VMEM)
    anywhere = pl.BlockSpec(memory_space=pltpu.HBM)
    out_shape = [jax.ShapeDtypeStruct((w, n), F32) for w in widths]
    if heads:
        out_shape.append(jax.ShapeDtypeStruct((heads, DH, DH), F32))
    count = len(slots)
    return pl.pallas_call(
        functools.partial(project_kernel, slots, len(start), heads),
        in_specs=[vmem] * len(start) + [anywhere] * (count + 2),
        out_specs=[vmem] * len(out_shape),
        out_shape=out_shape,
        scratch_shapes=[
            pltpu.VMEM((count, 4, cols, q), BF),
            pltpu.VMEM((count, 4, q, n), BF),
            pltpu.SemaphoreType.DMA((2 * count,)),
        ],
        cost_estimate=pl.CostEstimate(
            flops=8 * count * cols * q * n, bytes_accessed=8 * count * cols * q, transcendentals=0
        ),
        compiler_params=pltpu.CompilerParams(vmem_limit_bytes=limit << 20),
        name="project",
    )(*start, *weights, *hid)


def attend_kernel(pre_q, pre_k, pre_v, before, cot, own_grad, grad_att):
    pq = pre_q[...]
    pk = pre_k[...]
    q = (pq * sigmoid(pq)).astype(BF)
    k = (pk * sigmoid(pk)).astype(BF)
    v = pre_v[...].astype(BF)
    b = before[0].astype(BF)
    scores = jnp.where(causal_mask(q.shape[1]), dot(k, q, TN), 0.0).astype(BF)
    attended = dot(v, scores) + dot(b, q, TN)
    scale = lax.rsqrt(jnp.mean(attended * attended, axis=0, keepdims=True) + NORM_EPS)
    normed = attended * scale
    up = cot[...].T.astype(F32)
    ga = (scale * (up - normed * jnp.mean(up * normed, axis=0, keepdims=True))).astype(BF)
    grad_att[...] = ga
    own_grad[0] = dot(q, ga, NT)


def attend_back_kernel(pre_q, pre_k, pre_v, before, grad_att, back_q, grad_k, grad_v):
    pq = pre_q[...]
    pk = pre_k[...]
    q = (pq * sigmoid(pq)).astype(BF)
    k = (pk * sigmoid(pk)).astype(BF)
    v = pre_v[...].astype(BF)
    b = before[0].astype(BF)
    ga = grad_att[...]
    causal = causal_mask(q.shape[1])
    scores = jnp.where(causal, dot(k, q, TN), 0.0).astype(BF)
    gs = jnp.where(causal, dot(v, ga, TN), 0.0).astype(BF)
    gq = dot(k, gs) + dot(b, ga)
    back_q[...] = (gq * silu_slope(pq)).astype(BF)
    grad_k[...] = dot(q, gs, NT)
    grad_v[...] = dot(ga, scores, NT)


def head_specs(n, heads):
    row = pl.BlockSpec((DH, n), lambda h: (h, 0))
    row_v = pl.BlockSpec((DH, n), lambda h: (heads + h, 0))
    state = pl.BlockSpec((1, DH, DH), lambda h: (h, 0, 0))
    return row, row_v, state


def attend(pre_query, pre_kv, before, cotangent):
    width, n = pre_query.shape
    heads = width // DH
    row, row_v, state = head_specs(n, heads)
    return pl.pallas_call(
        attend_kernel,
        grid=(heads,),
        in_specs=[row, row, row_v, state, pl.BlockSpec((n, DH), lambda h: (0, h))],
        out_specs=[state, row],
        out_shape=[
            jax.ShapeDtypeStruct((heads, DH, DH), F32),
            jax.ShapeDtypeStruct((width, n), BF),
        ],
        compiler_params=pltpu.CompilerParams(vmem_limit_bytes=4 << 20),
        name="attend",
    )(pre_query, pre_kv, pre_kv, before, cotangent)


def attend_back(pre_query, pre_kv, before, grad_att):
    width, n = pre_query.shape
    heads = width // DH
    row, row_v, state = head_specs(n, heads)
    return pl.pallas_call(
        attend_back_kernel,
        grid=(heads,),
        in_specs=[row, row, row_v, state, row],
        out_specs=[row, row, row],
        out_shape=[
            jax.ShapeDtypeStruct((width, n), BF),
            jax.ShapeDtypeStruct((width, n), F32),
            jax.ShapeDtypeStruct((width, n), F32),
        ],
        cost_estimate=pl.CostEstimate(flops=6 * heads * n * n * DH, bytes_accessed=16 * n * width, transcendentals=0),
        compiler_params=pltpu.CompilerParams(vmem_limit_bytes=4 << 20),
        name="attend_back",
    )(pre_query, pre_kv, pre_kv, before, grad_att)


def row_table():
    x, c = lax.axis_index("x"), lax.axis_index("c")
    groups = []
    for oc in (1, 0):
        owner = c ^ oc
        for ox0, ox1 in ((0, 0), (3, 1), (1, 3), (2, 2)):
            groups.append((x ^ jnp.where(owner == 0, ox0, ox1)) * 2 + owner)
    return jnp.stack(groups).astype(jnp.int32)


def swap_rings(a, step):
    pairs = []
    for x in range(4):
        for c in range(2):
            pairs.append((x * 2 + c, (x ^ ((1, 3), (3, 1))[step][c]) * 2 + c))
    return lax.ppermute(a, ("x", "c"), pairs)


def chunk_copies(kind, srcs, bufs, sems):
    sides = [[(srcs[0], bufs[0])], [(src, buf) for src, buf in zip(srcs[1:], bufs[1:])]]
    pairs = []
    for i in range(4):
        at = pl.ds(2 * (i % 2), 2)
        pairs.append([pltpu.make_async_copy(s.at[at], b.at[at], sems.at[2 * i + j]) for j, (s, b) in enumerate(sides[i // 2])])
    return sides, pairs


def push_chunk(kind, rows, sides, pairs, outs, out_bufs, out_sems):
    half = rows.shape[0] // 2
    c = lax.axis_index("c")
    places = (c, 1 - c) if kind else (0, 1)
    leaving = []
    for i in range(4):
        for copy in pairs[i]:
            copy.wait()
        total, at = None, 0
        for _, buf in sides[i // 2]:
            side = jnp.concatenate([buf[2 * (i % 2)], buf[2 * (i % 2) + 1]], axis=1)
            term = dot(rows[:, at : at + side.shape[0]], side)
            total = term if total is None else total + term
            at += side.shape[0]
        cols = pl.ds(pl.multiple_of(places[i // 2] * 1024 + (i % 2) * 512, 512), 512)
        for j, part in enumerate((total[:half], total[half:])):
            out_bufs[j][i] = part.astype(out_bufs[j].dtype)
            leaving.append(pltpu.make_async_copy(out_bufs[j].at[i], outs[j].at[:, cols], out_sems.at[2 * i + j]))
            leaving[-1].start()
    return leaving


def collect_kernel(count, table, pre_kv, grad_k, grad_v, back_q, later, *refs):
    srcs, (rows_out, other, mine) = refs[:count], refs[count : count + 3]
    back = refs[count + 3]
    bufs = refs[count + 4 : 2 * count + 4]
    other_buf, mine_buf, sems, out_sems, rows, rows_sem = refs[2 * count + 4 :]
    sides, pairs = chunk_copies(0, srcs, bufs, sems)
    for pair in pairs:
        for copy in pair:
            copy.start()
    width, n = back_q.shape
    for h in range(width // DH):
        cols = slice(h * DH, (h + 1) * DH)
        vcols = slice(width + h * DH, width + (h + 1) * DH)
        qcols = slice(2 * width + h * DH, 2 * width + (h + 1) * DH)
        pk = pre_kv[cols, :]
        k = (pk * sigmoid(pk)).astype(BF)
        v = pre_kv[vcols, :].astype(BF)
        a = later[h].astype(BF)
        back[:, cols] = ((grad_k[cols, :] + dot(a, v)) * silu_slope(pk)).astype(BF).T
        back[:, vcols] = (grad_v[cols, :] + dot(a, k, TN)).astype(BF).T
        back[:, qcols] = back_q[cols, :].T
    g = n // 8
    for k in range(8):
        rows[k * g : (k + 1) * g, :] = back[pl.ds(pl.multiple_of(table[k] * g, g), g), :]
    leaving = [pltpu.make_async_copy(rows, rows_out, rows_sem)]
    leaving[0].start()
    leaving += push_chunk(0, rows, sides, pairs, (other, mine), (other_buf, mine_buf), out_sems)
    for copy in leaving:
        copy.wait()


def out_scratch(n):
    return [
        pltpu.VMEM((4, n // 2, 512), BF),
        pltpu.VMEM((4, n // 2, 512), BF),
        pltpu.SemaphoreType.DMA((8,)),
        pltpu.SemaphoreType.DMA((8,)),
    ]


def collect(pre_kv, grad_k, grad_v, back_q, later, weights):
    width, n = back_q.shape
    vmem = pl.BlockSpec(memory_space=pltpu.VMEM)
    hbm = pl.BlockSpec(memory_space=pltpu.HBM)
    return pl.pallas_call(
        functools.partial(collect_kernel, len(weights)),
        in_specs=[pl.BlockSpec(memory_space=pltpu.SMEM)] + [vmem] * 5 + [hbm] * len(weights),
        out_specs=[hbm] * 3,
        out_shape=[jax.ShapeDtypeStruct((n, 3 * width), BF)] + [jax.ShapeDtypeStruct((n // 2, 2048), BF)] * 2,
        scratch_shapes=[
            pltpu.VMEM((n, 3 * width), BF),
            *(pltpu.VMEM(w.shape, BF) for w in weights),
            *out_scratch(n),
            pltpu.VMEM((n, 3 * width), BF),
            pltpu.SemaphoreType.DMA,
        ],
        cost_estimate=pl.CostEstimate(flops=2 * n * 1536 * 2048, bytes_accessed=1536 * 4096, transcendentals=0),
        compiler_params=pltpu.CompilerParams(vmem_limit_bytes=54 << 20),
        name="collect",
    )(row_table(), pre_kv, grad_k, grad_v, back_q, later, *weights)


def push_kernel(kinds, counts, *refs):
    rows_in, srcs = refs[: len(kinds)], refs[len(kinds) : len(kinds) + sum(counts)]
    refs = refs[len(kinds) + sum(counts) :]
    outs, refs = refs[: 2 * len(kinds)], refs[2 * len(kinds) :]
    work = []
    for m, kind in enumerate(kinds):
        at = sum(counts[:m])
        rows, refs = refs[0], refs[1:]
        bufs, refs = refs[: counts[m]], refs[counts[m] :]
        (other_buf, mine_buf, sems, out_sems, rows_sem), refs = refs[:5], refs[5:]
        take_rows = pltpu.make_async_copy(rows_in[m], rows, rows_sem)
        take_rows.start()
        sides, pairs = chunk_copies(kind, srcs[at : at + counts[m]], bufs, sems)
        for pair in pairs:
            for copy in pair:
                copy.start()
        work.append((take_rows, kind, rows, sides, pairs, outs[2 * m : 2 * m + 2], (other_buf, mine_buf), out_sems))
    leaving = []
    for take_rows, *rest in work:
        take_rows.wait()
        leaving += push_chunk(*rest)
    for copy in leaving:
        copy.wait()


def push(share, kinds, rows, weights):
    n = rows[0].shape[0]
    hbm = pl.BlockSpec(memory_space=pltpu.HBM)
    loads = [2 * n * 1536 * 2048 // 100 * share for _ in kinds]
    counts = tuple(map(len, weights))
    scratch = []
    for r, ws in zip(rows, weights):
        scratch += [pltpu.VMEM(r.shape, BF), *(pltpu.VMEM(w.shape, BF) for w in ws), *out_scratch(n), pltpu.SemaphoreType.DMA]
    return pl.pallas_call(
        functools.partial(push_kernel, kinds, counts),
        in_specs=[hbm] * (len(kinds) + sum(counts)),
        out_specs=[hbm] * (2 * len(kinds)),
        out_shape=[jax.ShapeDtypeStruct((n // 2, 2048), BF)] * (2 * len(kinds)),
        scratch_shapes=scratch,
        cost_estimate=pl.CostEstimate(
            flops=int(sum(loads)), bytes_accessed=1, transcendentals=0
        ),
        compiler_params=pltpu.CompilerParams(vmem_limit_bytes=54 << 20),
        name="push",
    )(*rows, *(w for ws in weights for w in ws))


def transposed(w):
    return jnp.swapaxes(w.reshape(2, w.shape[0] // 2, w.shape[1]), 1, 2)


def on_device(hidden, w_query, w_key, w_value, cotangent):
    heads = w_query.shape[1] // DH
    n = hidden.shape[0]
    hid = reorder_columns(hidden, own_sources())
    block = jnp.concatenate([transposed(w_key), transposed(w_value), transposed(w_query)], axis=1)
    held, near, far, last_kv, last_q = gather(block, hid)
    wide = 2 * heads * DH
    sums = project(20, [held[0], near[0], held[1], near[1]], ((0, 0), (0, 4), (1, 0), (1, 4)), hid[0::3], (wide, wide // 2))
    sums = project(14, far, ((0, 0), (1, 0)), hid[1::3], (wide, wide // 2), sums)
    pre_kv, own_state = project(47, last_kv, ((0, 0), (1, 0)), hid[2::3], (wide,), sums[:1], heads)
    inner, total = state_round(own_state, "y", False)
    outer, _ = state_round(total, "z", False)
    before = inner + outer
    pre_query = project(44, last_q, ((0, 0), (1, 0)), hid[2::3], (wide // 2,), sums[1:])[0]
    own_grad, grad_att = attend(pre_query, pre_kv, before, cotangent)
    back_q, grad_k, grad_v = attend_back(pre_query, pre_kv, before, grad_att)
    inner, total = state_round(own_grad, "y", True)
    outer, _ = state_round(after(total, back_q), "z", True)
    later = inner + outer
    weights = [w for h in (0, 1) for w in ((held[h], last_kv[h], last_q[h]), (near[h], far[h]))]
    rows, *chunk = collect(pre_kv, grad_k, grad_v, back_q, later, weights[0])
    size = n // 8
    started = []
    for i in range(4):
        if i:
            use = rows
            if i == 2:
                use = after(rows, started[0][0])
            if i == 3:
                use = after(rows, started[1][0], started[0][1][0])
            chunk = push(100, (i % 2,), (use,), weights[i : i + 1])
        other, mine = chunk
        got = swap(other, "c", 1)
        send = (mine[2 * size :].astype(F32) + got[2 * size :].astype(F32)).astype(BF)
        got = mine[: 2 * size].astype(F32) + got[: 2 * size].astype(F32)
        got2 = swap_rings(send, 0)
        keep = got + got2.astype(F32)
        started.append((send, (got2, keep[size:].astype(BF)), keep))
    tables = []
    for h in (0, 1):
        src = sources(h, 0)
        for picks in ((0, 1, 2, 3, 12, 13, 14, 15), (4, 5, 6, 7, 8, 9, 10, 11)):
            tables.append(jnp.stack([src[p] for p in picks]))
    parts = []
    for i, (_, (_, send), keep) in enumerate(started):
        got = swap_rings(send, 1)
        if i < 2:
            got = after(got, started[2][0], started[3][0])
        parts.append(keep[:size] + got.astype(F32))
    return finish(parts, jnp.concatenate(tables).astype(jnp.int32))


def solution(mesh):
    finer = Mesh(mesh.devices.reshape(4, 4, 4, 2), ("z", "y", "x", "c"))
    in_specs = (P(SEQ, None), P(SEQ, HEAD), P(SEQ, HEAD), P(SEQ, HEAD), P(SEQ, HEAD))
    out_specs = P(SEQ + HEAD, None)
    return jax.shard_map(on_device, mesh=finer, in_specs=in_specs, out_specs=out_specs, check_vma=False)
```
